32 devices in a mesh: branch: 2 (over core), seq: 4 (over z), head: 4 (over y, x).
Axes of the slice: x: 2, y: 2, z: 4, core: 2. Of those that a mesh axis runs over, the one named last changes fastest.
Arguments:
- tokens: bfloat16 [1024, 3072], P('seq', 'head'), may hold values from -10 to 10
- valid_counts: int32 [4], P('seq'), may hold values from 1 to 256, 768 in all
- shared_qkv: bfloat16 [3072, 3, 1536], P('branch', None, 'head'), may hold values from -0.08479832 to 0.08479832
- shared_out: bfloat16 [1536, 3072], P('head', 'branch'), may hold values from -0.15625 to 0.15625
- skipped_qkv: bfloat16 [3072, 3, 1536], P('branch', None, 'head'), may hold values from -0.08479832 to 0.08479832
- skipped_out: bfloat16 [1536, 3072], P('head', 'branch'), may hold values from -0.15625 to 0.15625
- modulation: float32 [2, 3, 3072], replicated, may hold values from -3 to 3
- qk_gains: float32 [2, 2, 128], replicated, may hold values from 1.2 to 5.5
Outputs:
- branches: bfloat16 [2, 1024, 3072], P('branch', 'seq', 'head')
The draws below stay inside these ranges and needn't reach their ends.
Inputs may be any that keep to these rules, and one draw needn't show every extreme that they name: `valid_counts`: each entry counts the leading real tokens of one shard of 256 slots; the rest are padding. The entries sum to 768 and one of them equals 256.
All inputs are finite; a program needn't handle non-finite values.
Results may differ from the reference program's by a relative error of at most 0.01.
Values may be sent and summed in bfloat16 or wider, within the bound.
No kernel may reach another device: no remote copies, remote signals or barrier semaphores. Data moves between devices by JAX's collectives and lax.ppermute only.
A program may use at most 128 MiB of HBM per device.

```python
import math
import jax
import jax.numpy as jnp
import numpy as np
from jax import lax

D = 3072
HEADS = 12
HEAD_DIM = 128
SHARD = 256
TOKENS = 1024
N_SEQ = 4


def common_parts(key):
    base = jax.random.fold_in(key, 7001)
    first, second = jax.random.split(base)
    channel = jax.random.randint(first, (), 0, HEAD_DIM, dtype=jnp.int32)
    signs = (2 * jax.random.randint(second, (D,), 0, 2, dtype=jnp.int32) - 1).astype(jnp.float32)
    return (channel, signs)


def draw_tokens(key, part):
    signs = common_parts(key)[1]
    own = jax.random.fold_in(key, 11)
    first, second = jax.random.split(own)
    noise = jax.random.truncated_normal(first, -5.0, 5.0, (TOKENS, D), jnp.float32)
    strength = jax.random.uniform(second, (TOKENS, 1), jnp.float32, 1.0, 5.0)
    index = jnp.arange(TOKENS, dtype=jnp.int32)
    aligned = (index % 64 == 0)[:, None]
    values = noise + jnp.where(aligned, strength, 0.0) * signs[None, :]
    return values.astype(jnp.bfloat16)


def projection_draw(key, salt):
    channel, signs = common_parts(key)
    own = jax.random.fold_in(key, salt)
    shape = (D, 3, HEADS * HEAD_DIM)
    noise = jax.random.truncated_normal(own, -4.0, 4.0, shape, jnp.float32)
    column = jnp.arange(HEADS * HEAD_DIM, dtype=jnp.int32) % HEAD_DIM == channel
    which = jnp.arange(3, dtype=jnp.int32) < 2
    bump = jnp.where(which[:, None] & column[None, :], 0.7, 0.0)
    values = (noise + bump[None, :, :] * signs[:, None, None]) / jnp.sqrt(jnp.float32(D))
    return values.astype(jnp.bfloat16)


def draw_shared_qkv(key, part):
    return projection_draw(key, 21)


def draw_skipped_qkv(key, part):
    return projection_draw(key, 22)


def draw_qk_gains(key, part):
    channel = common_parts(key)[0]
    first, second = jax.random.split(jax.random.fold_in(key, 31))
    shape = (2, 2, HEAD_DIM)
    base = jnp.exp(jax.random.uniform(first, shape, jnp.float32, math.log(1.2), math.log(3.0)))
    high = jax.random.uniform(second, (2, 2, 1), jnp.float32, 5.0, 5.5)
    chosen = jnp.arange(HEAD_DIM, dtype=jnp.int32) == channel
    return jnp.where(chosen[None, None, :], high, base)


def steps_of(own_key, extent, pieces, low, largest):
    def one(axis_at, shards_of):
        heights = jax.random.uniform(jax.random.fold_in(jax.random.fold_in(own_key, 6), axis_at), (shards_of,), jnp.float32, low / len(pieces), largest / len(pieces))
        return jnp.repeat(jnp.exp(heights), extent[axis_at] // shards_of).reshape((-1,) + (1,) * (len(extent) - axis_at - 1))

    gain = one(*pieces[0])
    for cut in pieces[1:]:
        gain = gain * one(*cut)
    return gain


def length_profile(amount, total, bound, lean):
    portions = [(1 << 20) // math.isqrt(grade ** lean) + 1 for grade in range(2, amount + 1)]
    spare, given = total - bound - (amount - 1), [1] * (amount - 1)
    while spare > 0:
        movable = [i for i in range(amount - 1) if given[i] < bound]
        mass, budget = sum([portions[i] for i in movable]), spare
        for i in movable:
            addition = min(bound - given[i], max(1, budget * portions[i] // mass), spare)
            given[i] = given[i] + addition
            spare = spare - addition
    return np.array([bound] + given)


def ragged(rng, count, total, limit, skew):
    if count == 2:
        one = jax.random.randint(rng, (), max(1, total - limit), min(limit, total - 1) + 1)
        return jnp.stack([one, total - one])
    lengths = jnp.asarray(length_profile(count, total, limit, skew), jnp.int32)
    twos = (count - 1) // 2
    donor, receiver = lengths[1:1 + 2 * twos:2], lengths[2:2 + 2 * twos:2]
    slack = jnp.minimum(donor - 1, limit - receiver)
    shifted = jax.random.randint(jax.random.fold_in(rng, 1), (twos,), 0, 1 << 20) % (slack + 1)
    lengths = lengths.at[1:1 + 2 * twos:2].set(donor - shifted).at[2:2 + 2 * twos:2].set(receiver + shifted)
    return lengths[jax.random.permutation(jax.random.fold_in(rng, 2), count)]


def gaussian(stream_key, extent, spread, limit, shards=(), kind=jnp.bfloat16):
    entries = jax.random.normal(stream_key, extent, jnp.float32) * spread
    if len(shards) > 0:
        entries = steps_of(stream_key, extent, shards, -0.22, 0.18) * entries
    return jnp.clip(entries, min=-limit, max=limit).astype(kind)


def setup_inputs(seed: int = 0) -> dict:
    arg_keys = jax.random.split(jax.random.key(seed), 9)
    tokens = draw_tokens(jax.random.fold_in(arg_keys[8], 71), 0)
    valid_counts = ragged(arg_keys[1], N_SEQ, 3 * TOKENS // 4, SHARD, 1).astype(jnp.int32)
    shared_qkv = draw_shared_qkv(jax.random.fold_in(arg_keys[8], 71), 0)
    shared_out = gaussian(arg_keys[3], (HEADS * HEAD_DIM, D), (HEADS * HEAD_DIM) ** -0.5, 0.15625, ((0, 4), (1, 2)))
    skipped_qkv = draw_skipped_qkv(jax.random.fold_in(arg_keys[8], 71), 0)
    skipped_out = gaussian(arg_keys[5], (HEADS * HEAD_DIM, D), (HEADS * HEAD_DIM) ** -0.5, 0.15625, ((0, 4), (1, 2)))
    modulation = gaussian(arg_keys[6], (2, 3, D), 0.5, 3.0, (), jnp.float32)
    qk_gains = draw_qk_gains(jax.random.fold_in(arg_keys[8], 71), 0)
    return {"tokens": tokens, "valid_counts": valid_counts, "shared_qkv": shared_qkv, "shared_out": shared_out, "skipped_qkv": skipped_qkv, "skipped_out": skipped_out, "modulation": modulation, "qk_gains": qk_gains}


def run_block(x, qkv_weight, out_weight, mod, gains, keep):
    xf = x.astype(jnp.float32)
    mean = lax.optimization_barrier(jnp.mean(xf, axis=1, keepdims=True))
    centered = xf - mean
    var = lax.optimization_barrier(jnp.mean(centered * centered, axis=1, keepdims=True))
    normed = centered * lax.rsqrt(var + 1e-06)
    moded = (normed * (1.0 + mod[1]) + mod[0]).astype(jnp.bfloat16)
    qkv = jnp.einsum('td,dsc->tsc', moded.astype(jnp.float32), qkv_weight.astype(jnp.float32))
    count = x.shape[0]
    qpart = qkv[:, 0].reshape(count, HEADS, HEAD_DIM)
    kpart = qkv[:, 1].reshape(count, HEADS, HEAD_DIM)
    query = (qpart * lax.rsqrt(lax.optimization_barrier(jnp.mean(qpart * qpart, axis=2, keepdims=True)) + 1e-06) * gains[0]).astype(jnp.bfloat16)
    key = (kpart * lax.rsqrt(lax.optimization_barrier(jnp.mean(kpart * kpart, axis=2, keepdims=True)) + 1e-06) * gains[1]).astype(jnp.bfloat16)
    value = qkv[:, 2].reshape(count, HEADS, HEAD_DIM).astype(jnp.bfloat16)
    scale = 1.0 / HEAD_DIM ** 0.5

    def one_head(packed):
        qh, kh, vh = packed
        scores = jnp.dot(qh, kh.T, preferred_element_type=jnp.float32) * scale
        scores = jnp.where(keep[None, :], scores, -1e+30)
        peak = lax.optimization_barrier(jnp.max(scores, axis=1, keepdims=True))
        weights = jnp.where(keep[None, :], jnp.exp(scores - peak), 0.0)
        total = lax.optimization_barrier(jnp.sum(weights, axis=1, keepdims=True))
        mixed = jnp.dot(weights.astype(jnp.bfloat16), vh, preferred_element_type=jnp.float32)
        return (mixed / total).astype(jnp.bfloat16)
    attended = lax.map(one_head, (query.transpose(1, 0, 2), key.transpose(1, 0, 2), value.transpose(1, 0, 2)))
    attended = attended.transpose(1, 0, 2).reshape(count, HEADS * HEAD_DIM)
    projected = jnp.dot(attended, out_weight, preferred_element_type=jnp.float32)
    return (xf + mod[2] * projected).astype(jnp.bfloat16)

def reference(tokens, valid_counts, shared_qkv, shared_out, skipped_qkv, skipped_out, modulation, qk_gains):
    index = jnp.arange(TOKENS, dtype=jnp.int32)
    keep = index % SHARD < valid_counts[index // SHARD]
    forked = run_block(tokens, shared_qkv, shared_out, modulation[0], qk_gains[0], keep)
    strong = run_block(forked, skipped_qkv, skipped_out, modulation[1], qk_gains[1], keep)
    return jnp.stack([strong, forked])
```

```python
import jax
import jax.numpy as jnp
from jax import lax
from jax.sharding import PartitionSpec as P

HEAD_DIM = 128
EPS = 1e-06


def swap(x, axis, k, n):
    return lax.ppermute(x, axis, [(i, (i + k) % n) for i in range(n)])


def cross(x, axis, k, n):
    return lax.ppermute(x, axis, [(i, i ^ k) for i in range(n)])


def modulate(x, mod):
    xf = x.astype(jnp.float32)
    mean = jnp.mean(xf, axis=1, keepdims=True)
    centered = xf - mean
    var = jnp.mean(centered * centered, axis=1, keepdims=True)
    normed = centered * lax.rsqrt(var + EPS)
    return (normed * (1.0 + mod[1]) + mod[0]).astype(jnp.bfloat16)


def head_norm(part, gain):
    return (
        part * lax.rsqrt(jnp.mean(part * part, axis=2, keepdims=True) + EPS) * gain
    ).astype(jnp.bfloat16)


def block(x, counts, weights, outs, mod, gains, sizes):
    n_branch, n_seq, n_head = sizes
    b = lax.axis_index("branch")
    h = lax.axis_index("head")
    rows, quarter = x.shape
    width = weights[0].shape[2]
    group = width // HEAD_DIM
    pieces = [x] + [cross(x, "head", k, n_head) for k in range(1, n_head)]
    stacked = jnp.stack(pieces)
    whole = jnp.concatenate(
        [lax.dynamic_index_in_dim(stacked, j ^ h, 0, keepdims=False) for j in range(n_head)], axis=1
    )
    moded = modulate(whole, mod)
    depth = moded.shape[1] // 2
    mine = jnp.where(b == 0, moded[:, :depth], moded[:, depth:])
    other = jnp.where(b == 0, moded[:, depth:], moded[:, :depth])

    def project(lo, hi):
        n = (hi - lo) * width
        return jnp.dot(
            mine, weights[0][:, lo:hi].reshape(depth, n), preferred_element_type=jnp.float32
        ) + jnp.dot(
            other, weights[1][:, lo:hi].reshape(depth, n), preferred_element_type=jnp.float32
        )

    kv = project(1, 3)
    key = head_norm(kv[:, :width].reshape(rows, group, HEAD_DIM), gains[1]).reshape(rows, width)
    packed = jnp.concatenate([key, kv[:, width:].astype(jnp.bfloat16)], axis=1)
    query = head_norm(project(0, 1).reshape(rows, group, HEAD_DIM), gains[0])
    blocks = [packed] + [swap(packed, "seq", k, n_seq) for k in range(1, n_seq)]
    partner = [cross(p, "branch", 1, n_branch) for p in blocks]
    keys = jnp.concatenate(blocks + partner, axis=0)
    pos = jnp.arange(rows, dtype=jnp.int32)
    valid = jnp.concatenate(
        [b * rows + pos < c for c in counts] + [(1 - b) * rows + pos < c for c in counts]
    )[None, None, :]
    length = keys.shape[0]
    key_heads = keys[:, :width].reshape(length, group, HEAD_DIM)
    value_heads = keys[:, width:].reshape(length, group, HEAD_DIM)
    scale = 1.0 / HEAD_DIM**0.5
    scores = (
        jnp.einsum("rhd,nhd->hrn", query, key_heads, preferred_element_type=jnp.float32) * scale
    )
    scores = jnp.where(valid, scores, -1e30)
    peak = jnp.max(scores, axis=2, keepdims=True)
    weight = jnp.where(valid, jnp.exp(scores - peak), 0.0)
    total = jnp.sum(weight, axis=2)
    mixed = jnp.einsum(
        "hrn,nhd->hrd",
        weight.astype(jnp.bfloat16),
        value_heads,
        preferred_element_type=jnp.float32,
    )
    attended = (mixed / total[:, :, None]).astype(jnp.bfloat16)
    attended = attended.transpose(1, 0, 2).reshape(rows, width)
    left = jnp.dot(attended, outs[0], preferred_element_type=jnp.float32)
    right = jnp.dot(attended, outs[1], preferred_element_type=jnp.float32)
    projected = jnp.concatenate(
        [jnp.where(b == 0, left, right), jnp.where(b == 0, right, left)], axis=1
    )
    total_out = lax.dynamic_slice_in_dim(projected, h * quarter, quarter, 1)
    for k in range(1, n_head):
        part = lax.dynamic_slice_in_dim(projected, (h ^ k) * quarter, quarter, 1)
        total_out = total_out + cross(part.astype(jnp.bfloat16), "head", k, n_head).astype(
            jnp.float32
        )
    gate = lax.dynamic_slice_in_dim(mod[2], h * quarter, quarter, 0)
    return (x.astype(jnp.float32) + gate[None, :] * total_out).astype(jnp.bfloat16)


def solution(mesh):
    n_branch, n_seq, n_head = (mesh.shape[a] for a in ("branch", "seq", "head"))
    sizes = (n_branch, n_seq, n_head)

    def per_device(
        tokens, valid_counts, shared_qkv, shared_out, skipped_qkv, skipped_out, modulation, qk_gains
    ):
        b = lax.axis_index("branch")
        rows = tokens.shape[0] // n_branch
        x = lax.dynamic_slice_in_dim(tokens, b * rows, rows, 0)
        count = valid_counts.astype(jnp.float32)
        counts = [valid_counts[0]] + [
            swap(count, "seq", k, n_seq)[0].astype(jnp.int32) for k in range(1, n_seq)
        ]
        both = lambda w: (w, cross(w, "branch", 1, n_branch))
        w0, o0, w1, o1 = both(shared_qkv), both(shared_out), both(skipped_qkv), both(skipped_out)
        forked = block(x, counts, w0, o0, modulation[0], qk_gains[0], sizes)
        strong = block(forked, counts, w1, o1, modulation[1], qk_gains[1], sizes)
        got = cross(jnp.where(b == 0, forked, strong), "branch", 1, n_branch)
        low = jnp.where(b == 0, strong, got)
        high = jnp.where(b == 0, got, forked)
        return jnp.concatenate([low, high], axis=0)[None]

    in_specs = (
        P("seq", "head"),
        P("seq"),
        P("branch", None, "head"),
        P("head", "branch"),
        P("branch", None, "head"),
        P("head", "branch"),
        P(),
        P(),
    )
    return jax.shard_map(
        per_device,
        mesh=mesh,
        in_specs=in_specs,
        out_specs=P("branch", "seq", "head"),
        check_vma=False,
    )
```

```python
import functools

import jax
import jax.numpy as jnp
from jax import lax
from jax.experimental import pallas as pl
from jax.experimental.pallas import tpu as pltpu
from jax.sharding import PartitionSpec as P

HEAD_DIM = 128
EPS = 1e-06
F32 = jnp.float32
BF16 = jnp.bfloat16
VMEM = pl.BlockSpec(memory_space=pltpu.VMEM)
SMEM = pl.BlockSpec(memory_space=pltpu.SMEM)
ANY = pl.BlockSpec(memory_space=pl.ANY)
MIB = 1 << 20


def turn(x, axis, k, n):
    return lax.ppermute(x, axis, [(i, (i + k) % n) for i in range(n)])


def cross(x, axis, k, n):
    return lax.ppermute(x, axis, [(i, i ^ k) for i in range(n)])


def params(mib):
    return pltpu.CompilerParams(vmem_limit_bytes=mib * MIB)


def half_kernel(tok_ref, out_ref, sem):
    rows = out_ref.shape[0]
    start = pl.multiple_of(lax.axis_index("branch") * rows, rows)
    copy = pltpu.make_async_copy(tok_ref.at[pl.ds(start, rows)], out_ref, sem)
    copy.start()
    copy.wait()


def take_half(tokens, n_branch):
    rows, cols = tokens.shape
    return pl.pallas_call(
        half_kernel,
        out_shape=jax.ShapeDtypeStruct((rows // n_branch, cols), tokens.dtype),
        in_specs=[ANY],
        out_specs=VMEM,
        scratch_shapes=[pltpu.SemaphoreType.DMA],
        compiler_params=params(4),
        name="take_half",
    )(tokens)


def contract(moded_ref, own_ref, other_ref, which, n_head):
    b = lax.axis_index("branch")
    h = lax.axis_index("head")
    quarter = moded_ref.shape[2]
    per_core = n_head // 2
    total = None
    for ref, core in ((own_ref, b), (other_ref, 1 - b)):
        for i in range(per_core):
            piece = moded_ref[(core * per_core + i) ^ h]
            term = jnp.dot(
                piece,
                ref[which, i * quarter : (i + 1) * quarter, :],
                preferred_element_type=F32,
            )
            total = term if total is None else total + term
    return total


def norm_heads(part, gain, width):
    outs = []
    for lo in range(0, width, HEAD_DIM):
        one = part[:, lo : lo + HEAD_DIM]
        scale = lax.rsqrt(jnp.mean(one * one, axis=1, keepdims=True) + EPS)
        outs.append((one * scale * gain).astype(BF16))
    return outs


def kv_kernel(blk, n_head, *refs):
    xs = refs[:n_head]
    own_ref, other_ref, mod_ref, gain_ref, packed_ref, moded_ref = refs[n_head:]
    h = lax.axis_index("head")
    quarter = xs[0].shape[1]
    width = own_ref.shape[2]
    total = sum(jnp.sum(x[...].astype(F32), axis=1, keepdims=True) for x in xs)
    mean = total / (n_head * quarter)
    square = 0.0
    for x in xs:
        centered = x[...].astype(F32) - mean
        square = square + jnp.sum(centered * centered, axis=1, keepdims=True)
    scale = lax.rsqrt(square / (n_head * quarter) + EPS)
    for k, x in enumerate(xs):
        at = pl.ds(pl.multiple_of((h ^ k) * quarter, quarter), quarter)
        shift = mod_ref[0, blk : blk + 1, at]
        gain = mod_ref[1, blk : blk + 1, at] + 1.0
        normed = (x[...].astype(F32) - mean) * scale
        moded_ref[k] = (normed * gain + shift).astype(BF16)
    key = contract(moded_ref, own_ref, other_ref, 1, n_head)
    for i, out in enumerate(norm_heads(key, gain_ref[blk, 1:2, :], width)):
        packed_ref[:, i * HEAD_DIM : (i + 1) * HEAD_DIM] = out
    packed_ref[:, width:] = contract(moded_ref, own_ref, other_ref, 2, n_head).astype(BF16)


def q_kernel(blk, n_head, moded_ref, own_ref, other_ref, gain_ref, query_ref):
    width = own_ref.shape[2]
    query = contract(moded_ref, own_ref, other_ref, 0, n_head)
    for i, out in enumerate(norm_heads(query, gain_ref[blk, 0:1, :], width)):
        query_ref[:, i * HEAD_DIM : (i + 1) * HEAD_DIM] = out


def attend_kernel(n_seq, n_head, *refs):
    query_ref = refs[0]
    blocks = refs[1 : 1 + 2 * n_seq]
    counts = refs[1 + 2 * n_seq : 1 + 3 * n_seq]
    own_ref, other_ref = refs[1 + 3 * n_seq : 3 + 3 * n_seq]
    outs = refs[3 + 3 * n_seq : 3 + 3 * n_seq + n_head]
    attended, spread = refs[3 + 3 * n_seq + n_head :]
    b = lax.axis_index("branch")
    h = lax.axis_index("head")
    rows, width = query_ref.shape
    scale = 1.0 / HEAD_DIM**0.5
    lane = lax.broadcasted_iota(jnp.int32, (1, rows), 1)
    valid = []
    for i in range(2 * n_seq):
        core = b if i < n_seq else 1 - b
        valid.append(lane + core * rows < counts[i % n_seq][0])
    for lo in range(0, width, HEAD_DIM):
        at = slice(lo, lo + HEAD_DIM)
        query = query_ref[:, at]
        scores = []
        for block, ok in zip(blocks, valid):
            one = lax.dot_general(
                query, block[:, at], (((1,), (1,)), ((), ())), preferred_element_type=F32
            )
            scores.append(jnp.where(ok, one * scale, -1e30))
        peak = functools.reduce(jnp.maximum, scores)
        peak = jnp.max(peak, axis=1, keepdims=True)
        mixed = None
        total = None
        for block, ok, one in zip(blocks, valid, scores):
            weight = jnp.where(ok, jnp.exp(one - peak), 0.0)
            total = weight if total is None else total + weight
            term = jnp.dot(
                weight.astype(BF16),
                block[:, width + lo : width + lo + HEAD_DIM],
                preferred_element_type=F32,
            )
            mixed = term if mixed is None else mixed + term
        total = jnp.sum(total, axis=1, keepdims=True)
        attended[:, at] = (mixed / total).astype(BF16)
    quarter = outs[0].shape[1]
    per_core = n_head // 2
    value = attended[...]
    for ref, core in ((own_ref, b), (other_ref, 1 - b)):
        for i in range(per_core):
            spread[(core * per_core + i) ^ h] = jnp.dot(
                value, ref[:, i * quarter : (i + 1) * quarter], preferred_element_type=F32
            )
    for k, out in enumerate(outs):
        out[...] = spread[k].astype(out.dtype)


def join_kernel(blk, n_head, *refs):
    x_ref, kept_ref = refs[:2]
    parts = refs[2 : 1 + n_head]
    mod_ref, out_ref = refs[1 + n_head :]
    h = lax.axis_index("head")
    quarter = x_ref.shape[1]
    gate = mod_ref[2, blk : blk + 1, pl.ds(pl.multiple_of(h * quarter, quarter), quarter)]
    total = kept_ref[...]
    for part in parts:
        total = total + part[...].astype(F32)
    out_ref[...] = (x_ref[...].astype(F32) + gate * total).astype(BF16)


def block(x, counts, weights, outs, mod, gains, blk, sizes):
    n_branch, n_seq, n_head = sizes
    rows, quarter = x.shape
    width = weights[0].shape[2]
    shape = jax.ShapeDtypeStruct
    pieces = [x] + [cross(x, "head", k, n_head) for k in range(1, n_head)]
    packed, moded = pl.pallas_call(
        functools.partial(kv_kernel, blk, n_head),
        out_shape=(shape((rows, 2 * width), BF16), shape((n_head, rows, quarter), BF16)),
        in_specs=[VMEM] * (n_head + 4),
        out_specs=(VMEM, VMEM),
        compiler_params=params(24),
        name=f"kv_{blk}",
    )(*pieces, *weights, mod, gains)
    blocks = [packed] + [turn(packed, "seq", k, n_seq) for k in range(1, n_seq)]
    query = pl.pallas_call(
        functools.partial(q_kernel, blk, n_head),
        out_shape=shape((rows, width), BF16),
        in_specs=[VMEM] * 4,
        out_specs=VMEM,
        compiler_params=params(24),
        name=f"q_{blk}",
    )(moded, *weights, gains)
    partner = [cross(p, "branch", 1, n_branch) for p in blocks]
    sent = pl.pallas_call(
        functools.partial(attend_kernel, n_seq, n_head),
        out_shape=tuple(
            shape((rows, quarter), F32 if k == 0 else BF16) for k in range(n_head)
        ),
        in_specs=[VMEM] * (1 + 2 * n_seq) + [SMEM] * n_seq + [VMEM] * 2,
        out_specs=tuple([VMEM] * n_head),
        scratch_shapes=[
            pltpu.VMEM((rows, width), BF16),
            pltpu.VMEM((n_head, rows, quarter), F32),
        ],
        compiler_params=params(24),
        name=f"attend_{blk}",
    )(query, *blocks, *partner, *counts, *outs)
    parts = [cross(sent[k], "head", k, n_head) for k in range(1, n_head)]
    return pl.pallas_call(
        functools.partial(join_kernel, blk, n_head),
        out_shape=shape((rows, quarter), BF16),
        in_specs=[VMEM] * (n_head + 2),
        out_specs=VMEM,
        compiler_params=params(8),
        name=f"join_{blk}",
    )(x, sent[0], *parts, mod)


def solution(mesh):
    n_branch, n_seq, n_head = (mesh.shape[a] for a in ("branch", "seq", "head"))
    sizes = (n_branch, n_seq, n_head)

    def per_device(
        tokens, valid_counts, shared_qkv, shared_out, skipped_qkv, skipped_out, modulation, qk_gains
    ):
        b = lax.axis_index("branch")
        x = take_half(tokens, n_branch)
        counts = [valid_counts] + [turn(valid_counts, "seq", k, n_seq) for k in range(1, n_seq)]
        both = lambda w: (w, cross(w, "branch", 1, n_branch))
        first = both(shared_qkv.transpose(1, 0, 2))
        second = both(skipped_qkv.transpose(1, 0, 2))
        mod = modulation.transpose(1, 0, 2)
        forked = block(x, counts, first, both(shared_out), mod, qk_gains, 0, sizes)
        strong = block(forked, counts, second, both(skipped_out), mod, qk_gains, 1, sizes)
        got = cross(jnp.where(b == 0, forked, strong), "branch", 1, n_branch)
        low = jnp.where(b == 0, strong, got)
        high = jnp.where(b == 0, got, forked)
        return jnp.concatenate([low, high], axis=0)[None]

    in_specs = (
        P("seq", "head"),
        P("seq"),
        P("branch", None, "head"),
        P("head", "branch"),
        P("branch", None, "head"),
        P("head", "branch"),
        P(),
        P(),
    )
    return jax.shard_map(
        per_device,
        mesh=mesh,
        in_specs=in_specs,
        out_specs=P("branch", "seq", "head"),
        check_vma=False,
    )
```

```python
import functools
import math

import jax
import jax.numpy as jnp
from jax import lax
from jax.experimental import pallas as pl
from jax.experimental.pallas import tpu as pltpu
from jax.sharding import PartitionSpec as P


HEAD_DIM = 128
EPS = 1e-06
F32 = jnp.float32
BF16 = jnp.bfloat16
VMEM = pl.BlockSpec(memory_space=pltpu.VMEM)
SMEM = pl.BlockSpec(memory_space=pltpu.SMEM)
FAR = pl.BlockSpec(memory_space=pl.ANY)
MIB = 1 << 20
SHAPE = jax.ShapeDtypeStruct


def turn(x, axis, k, n):
    return lax.ppermute(x, axis, [(i, (i + k) % n) for i in range(n)])


def cross(x, axis, k, n):
    return lax.ppermute(x, axis, [(i, i ^ k) for i in range(n)])


def swap(x):
    return lax.ppermute(x, "branch", [(0, 1), (1, 0)])


def far(x):
    return pltpu.with_memory_space_constraint(x, pltpu.HBM)


def params(mib):
    return pltpu.CompilerParams(vmem_limit_bytes=mib * MIB)


def half_kernel(tok_ref, out_ref, sem):
    rows = out_ref.shape[0]
    start = pl.multiple_of(lax.axis_index("branch") * rows, rows)
    copy = pltpu.make_async_copy(tok_ref.at[pl.ds(start, rows)], out_ref, sem)
    copy.start()
    copy.wait()


def take_half(tokens, n_branch):
    rows, cols = tokens.shape
    return pl.pallas_call(
        half_kernel,
        out_shape=SHAPE((rows // n_branch, cols), tokens.dtype),
        in_specs=[FAR],
        out_specs=VMEM,
        scratch_shapes=[pltpu.SemaphoreType.DMA],
        compiler_params=params(4),
        name="take_half",
    )(far(tokens))


def prep_kernel(n_head, *refs):
    far_qkv, near_ref, across_ref, far_mod, far_gain = refs[:5]
    qkv_ref, mod_ref, gain_ref = refs[5:8]
    pieces = refs[8 : 9 + n_head]
    sems = refs[9 + n_head]
    copies = [
        pltpu.make_async_copy(src, dst, sems.at[i])
        for i, (src, dst) in enumerate(
            ((far_qkv, qkv_ref), (far_mod, mod_ref), (far_gain, gain_ref))
        )
    ]
    for copy in copies:
        copy.start()
    b = lax.axis_index("branch")
    h = lax.axis_index("head")
    per_core = n_head // 2
    part = pieces[0].shape[1]
    for k in range(n_head + 1):
        j = h ^ (k % n_head)
        half = b if k < n_head else 1 - b
        at = pl.ds(pl.multiple_of(lax.rem(j, per_core) * 2 * part + half * part, part), part)
        mine = lax.div(j, per_core) == b
        piece = pieces[k]

        @pl.when(mine)
        def _():
            piece[...] = near_ref[:, at]

        @pl.when(jnp.logical_not(mine))
        def _():
            piece[...] = across_ref[:, at]

    for copy in copies:
        copy.wait()


def contract(moded_ref, own_ref, other_ref, which, n_head):
    b = lax.axis_index("branch")
    h = lax.axis_index("head")
    quarter = moded_ref.shape[2]
    per_core = n_head // 2
    total = None
    for ref, core in ((own_ref, b), (other_ref, 1 - b)):
        for i in range(per_core):
            piece = moded_ref[(core * per_core + i) ^ h]
            term = jnp.dot(
                piece,
                ref[which, i * quarter : (i + 1) * quarter, :],
                preferred_element_type=F32,
            )
            total = term if total is None else total + term
    return total


def norm_heads(part, gain, width):
    outs = []
    for lo in range(0, width, HEAD_DIM):
        one = part[:, lo : lo + HEAD_DIM]
        scale = lax.rsqrt(jnp.mean(one * one, axis=1, keepdims=True) + EPS)
        outs.append((one * scale * gain).astype(BF16))
    return outs


def kv_kernel(blk, n_head, *refs):
    xs = refs[:n_head]
    own_ref, other_ref, mod_ref, gain_ref, packed_ref, moded_ref = refs[n_head:]
    h = lax.axis_index("head")
    quarter = xs[0].shape[1]
    width = own_ref.shape[2]
    total = sum(jnp.sum(x[...].astype(F32), axis=1, keepdims=True) for x in xs)
    mean = total / (n_head * quarter)
    square = 0.0
    for x in xs:
        centered = x[...].astype(F32) - mean
        square = square + jnp.sum(centered * centered, axis=1, keepdims=True)
    scale = lax.rsqrt(square / (n_head * quarter) + EPS)
    for k, x in enumerate(xs):
        at = pl.ds(pl.multiple_of((h ^ k) * quarter, quarter), quarter)
        shift = mod_ref[0, blk : blk + 1, at]
        gain = mod_ref[1, blk : blk + 1, at] + 1.0
        normed = (x[...].astype(F32) - mean) * scale
        moded_ref[k] = (normed * gain + shift).astype(BF16)
    key = contract(moded_ref, own_ref, other_ref, 1, n_head)
    for i, out in enumerate(norm_heads(key, gain_ref[blk, 1:2, :], width)):
        packed_ref[:, i * HEAD_DIM : (i + 1) * HEAD_DIM] = out
    packed_ref[:, width:] = contract(moded_ref, own_ref, other_ref, 2, n_head).astype(BF16)


def q_kernel(blk, n_head, moded_ref, own_ref, other_ref, gain_ref, query_ref):
    width = own_ref.shape[2]
    query = contract(moded_ref, own_ref, other_ref, 0, n_head)
    for i, out in enumerate(norm_heads(query, gain_ref[blk, 0:1, :], width)):
        query_ref[:, i * HEAD_DIM : (i + 1) * HEAD_DIM] = out


def drop_kernel(n_seq, *refs):
    counts, out_ref = refs[:n_seq], refs[n_seq]
    b = lax.axis_index("branch")
    rows = out_ref.shape[1]
    lane = lax.broadcasted_iota(jnp.int32, (1, rows), 1)
    for i in range(2 * n_seq):
        core = b if i < n_seq else 1 - b
        out_ref[i : i + 1, :] = jnp.where(
            lane + core * rows < counts[i % n_seq][0], 0.0, -1e30
        ).astype(F32)


def scan_keys(query, at, pairs, drop_ref):
    scale = math.log2(math.e) / HEAD_DIM**0.5
    scores = []
    for ref, i in pairs:
        one = lax.dot_general(
            query, ref[:, at], (((1,), (1,)), ((), ())), preferred_element_type=F32
        )
        scores.append(one * scale + drop_ref[i : i + 1, :])
    return scores


def weigh(scores, peak, pairs, width, lo):
    mixed = None
    total = None
    for one, (ref, _) in zip(scores, pairs):
        weight = jnp.exp2(one - peak)
        total = weight if total is None else total + weight
        term = jnp.dot(
            weight.astype(BF16),
            ref[:, width + lo : width + lo + HEAD_DIM],
            preferred_element_type=F32,
        )
        mixed = term if mixed is None else mixed + term
    return mixed, jnp.sum(total, axis=1, keepdims=True)


def key_pairs(blocks, order, n_seq):
    n = len(order)
    return [(blocks[i], order[i]) for i in range(n)] + [
        (blocks[n + i], n_seq + order[i]) for i in range(n)
    ]


def first_kernel(order, n_seq, *refs):
    query_ref = refs[0]
    n = 2 * len(order)
    blocks, drop_ref = refs[1 : 1 + n], refs[1 + n]
    mixed_ref, stat_ref = refs[2 + n :]
    width = query_ref.shape[1]
    pairs = key_pairs(blocks, order, n_seq)
    for i, lo in enumerate(range(0, width, HEAD_DIM)):
        at = slice(lo, lo + HEAD_DIM)
        scores = scan_keys(query_ref[:, at], at, pairs, drop_ref)
        peak = jnp.max(functools.reduce(jnp.maximum, scores), axis=1, keepdims=True)
        mixed, total = weigh(scores, peak, pairs, width, lo)
        mixed_ref[:, at] = mixed
        stat_ref[0, :, i : i + 1] = peak
        stat_ref[1, :, i : i + 1] = total


def last_kernel(order, n_seq, *refs):
    query_ref = refs[0]
    n = 2 * len(order)
    blocks, drop_ref = refs[1 : 1 + n], refs[1 + n]
    mixed_ref, stat_ref, out_ref = refs[2 + n :]
    width = query_ref.shape[1]
    pairs = key_pairs(blocks, order, n_seq)
    for i, lo in enumerate(range(0, width, HEAD_DIM)):
        at = slice(lo, lo + HEAD_DIM)
        scores = scan_keys(query_ref[:, at], at, pairs, drop_ref)
        before = stat_ref[0, :, i : i + 1]
        peak = jnp.max(functools.reduce(jnp.maximum, scores), axis=1, keepdims=True)
        peak = jnp.maximum(peak, before)
        mixed, total = weigh(scores, peak, pairs, width, lo)
        keep = jnp.exp2(before - peak)
        mixed = mixed + mixed_ref[:, at] * keep
        total = total + stat_ref[1, :, i : i + 1] * keep
        out_ref[:, at] = (mixed / total).astype(BF16)


def out_kernel(blk, n_head, *refs):
    attended = refs[:n_head]
    mine = refs[n_head : 2 * n_head]
    others = refs[2 * n_head : 3 * n_head]
    x_ref, mod_ref, out_ref = refs[3 * n_head :]
    b = lax.axis_index("branch")
    h = lax.axis_index("head")
    quarter = x_ref.shape[1]
    part = mine[0].shape[1]
    for weights, core in ((mine, b), (others, 1 - b)):
        total = None
        for value, weight in zip(attended, weights):
            term = jnp.dot(value[...], weight[...], preferred_element_type=F32)
            total = term if total is None else total + term
        start = pl.multiple_of(core * part, part)
        at = pl.ds(pl.multiple_of(h * quarter + start, part), part)
        here = pl.ds(start, part)
        gate = mod_ref[2, blk : blk + 1, at]
        out_ref[:, here] = (x_ref[:, here].astype(F32) + gate * total).astype(BF16)


def join_kernel(strong_ref, forked_ref, got_ref, out_ref):
    b = lax.axis_index("branch")
    rows = strong_ref.shape[0]

    @pl.when(b == 0)
    def _():
        out_ref[:rows, :] = strong_ref[...]
        out_ref[rows:, :] = got_ref[...]

    @pl.when(b != 0)
    def _():
        out_ref[:rows, :] = got_ref[...]
        out_ref[rows:, :] = forked_ref[...]


def block(tokens, x, valid, weights, outs, mod, gains, blk, sizes, later):
    n_branch, n_seq, n_head = sizes
    if blk == 0:
        weights = (weights, swap(weights))
        outs = (outs, swap(outs))
        x = take_half(tokens, n_branch)
    rows, quarter = x.shape
    width = weights[0].shape[2]
    part = quarter // n_branch
    pieces = [x] + [cross(x, "head", k, n_head) for k in range(1, n_head)]
    if blk == 0:
        valid = [valid] + [turn(valid, "seq", k, n_seq) for k in range(1, n_seq)]
        valid = pl.pallas_call(
            functools.partial(drop_kernel, n_seq),
            out_shape=SHAPE((2 * n_seq, rows), F32),
            in_specs=[SMEM] * n_seq,
            out_specs=VMEM,
            compiler_params=params(4),
            name="drop",
        )(*valid)
    own, mod, gains, *spread = pl.pallas_call(
        functools.partial(prep_kernel, n_head),
        out_shape=[SHAPE(weights[0].shape, BF16), SHAPE(mod.shape, F32), SHAPE(gains.shape, F32)]
        + [SHAPE((width, part), BF16)] * (n_head + 1),
        in_specs=[FAR, VMEM, VMEM, FAR, FAR],
        out_specs=[VMEM] * (n_head + 4),
        scratch_shapes=[pltpu.SemaphoreType.DMA((3,))],
        compiler_params=params(16),
    )(far(weights[0]), *outs, far(mod), far(gains))
    weights = (own, weights[1])
    packed, moded = pl.pallas_call(
        functools.partial(kv_kernel, blk, n_head),
        out_shape=(SHAPE((rows, 2 * width), BF16), SHAPE((n_head, rows, quarter), BF16)),
        in_specs=[VMEM] * (n_head + 4),
        out_specs=(VMEM, VMEM),
        compiler_params=params(16),
    )(*pieces, *weights, mod, gains)
    blocks = [packed] + [turn(packed, "seq", k, n_seq) for k in range(1, n_seq)]
    mine = [spread[0]] + [cross(spread[k], "head", k, n_head) for k in range(1, n_head)]
    query = pl.pallas_call(
        functools.partial(q_kernel, blk, n_head),
        out_shape=SHAPE((rows, width), BF16),
        in_specs=[VMEM] * 4,
        out_specs=VMEM,
        compiler_params=params(16),
    )(moded, *weights, gains)
    if blk == 0:
        qkv, out_weight = later
        later = ((qkv, swap(qkv)), (out_weight, swap(out_weight)))
    partner = [swap(p) for p in blocks]
    others = [spread[n_head]] + [swap(p) for p in mine[1:]]
    cut = max(1, n_seq // 2)
    early, late = tuple(range(cut)), tuple(range(cut, n_seq))
    pick = lambda which: [blocks[i] for i in which] + [partner[i] for i in which]
    mixed, stat = pl.pallas_call(
        functools.partial(first_kernel, early, n_seq),
        out_shape=(SHAPE((rows, width), F32), SHAPE((2, rows, HEAD_DIM), F32)),
        in_specs=[VMEM] * (2 + 2 * len(early)),
        out_specs=(VMEM, VMEM),
        compiler_params=params(16),
    )(query, *pick(early), valid)
    attended = pl.pallas_call(
        functools.partial(last_kernel, late, n_seq),
        out_shape=SHAPE((rows, width), BF16),
        in_specs=[VMEM] * (4 + 2 * len(late)),
        out_specs=VMEM,
        compiler_params=params(16),
    )(query, *pick(late), valid, mixed, stat)
    gathered = [attended] + [cross(attended, "head", k, n_head) for k in range(1, n_head)]
    out = pl.pallas_call(
        functools.partial(out_kernel, blk, n_head),
        out_shape=SHAPE((rows, quarter), BF16),
        in_specs=[VMEM] * (3 * n_head + 2),
        out_specs=VMEM,
        compiler_params=params(16),
    )(*gathered, *mine, *others, x, mod)
    return out, valid, later


def solution(mesh):
    sizes = tuple(mesh.shape[a] for a in ("branch", "seq", "head"))

    def per_device(
        tokens, valid_counts, shared_qkv, shared_out, skipped_qkv, skipped_out, modulation, qk_gains
    ):
        b = lax.axis_index("branch")
        mod = modulation.transpose(1, 0, 2)
        later = skipped_qkv.transpose(1, 0, 2), skipped_out
        forked, valid, later = block(
            tokens, None, valid_counts, shared_qkv.transpose(1, 0, 2), shared_out, mod,
            qk_gains, 0, sizes, later,
        )
        strong, _, _ = block(None, forked, valid, *later, mod, qk_gains, 1, sizes, None)
        got = swap(jnp.where(b == 0, forked, strong))
        rows, quarter = strong.shape
        out = pl.pallas_call(
            join_kernel,
            out_shape=SHAPE((2 * rows, quarter), BF16),
            in_specs=[VMEM] * 3,
            out_specs=VMEM,
            compiler_params=params(8),
            name="join",
        )(strong, forked, got)
        return out[None]

    in_specs = (
        P("seq", "head"),
        P("seq"),
        P("branch", None, "head"),
        P("head", "branch"),
        P("branch", None, "head"),
        P("head", "branch"),
        P(),
        P(),
    )
    return jax.shard_map(
        per_device,
        mesh=mesh,
        in_specs=in_specs,
        out_specs=P("branch", "seq", "head"),
        check_vma=False,
    )
```

```python
import functools
import math

import jax
import jax.numpy as jnp
from jax import lax
from jax.experimental import pallas as pl
from jax.experimental.pallas import tpu as pltpu
from jax.sharding import PartitionSpec as P


HEAD_DIM = 128
EPS = 1e-06
MARK = 1e4
MARK_SUM = 1e5
F32 = jnp.float32
BF16 = jnp.bfloat16
VMEM = pl.BlockSpec(memory_space=pltpu.VMEM)
SMEM = pl.BlockSpec(memory_space=pltpu.SMEM)
FAR = pl.BlockSpec(memory_space=pl.ANY)
MIB = 1 << 20
SHAPE = jax.ShapeDtypeStruct


def turn(x, axis, k, n):
    return lax.ppermute(x, axis, [(i, (i + k) % n) for i in range(n)])


def cross(x, axis, k, n):
    return lax.ppermute(x, axis, [(i, i ^ k) for i in range(n)])


def swap(x):
    return lax.ppermute(x, "branch", [(0, 1), (1, 0)])


def far(x):
    return pltpu.with_memory_space_constraint(x, pltpu.HBM)


def params(mib):
    return pltpu.CompilerParams(vmem_limit_bytes=mib * MIB)


def half_kernel(tok_ref, *refs):
    outs, sem = refs[:-1], refs[-1]
    rows = outs[0].shape[0]
    start = pl.multiple_of(lax.axis_index("branch") * len(outs) * rows, rows)
    copies = [
        pltpu.make_async_copy(tok_ref.at[pl.ds(start + i * rows, rows)], out, sem.at[i])
        for i, out in enumerate(outs)
    ]
    for copy in copies:
        copy.start()
    for copy in copies:
        copy.wait()


def take_half(tokens, n_branch, chunks):
    rows, cols = tokens.shape
    return pl.pallas_call(
        half_kernel,
        out_shape=[SHAPE((rows // n_branch // chunks, cols), tokens.dtype)] * chunks,
        in_specs=[FAR],
        out_specs=[VMEM] * chunks,
        scratch_shapes=[pltpu.SemaphoreType.DMA((chunks,))],
        compiler_params=params(4),
        name="take_half",
    )(far(tokens))


def prep_kernel(marks, *refs):
    far_qkv, far_mod, far_gain = refs[:3]
    rest = refs[3:]
    if marks:
        count_ref, rest = rest[0], rest[1:]
    qkv_ref, mod_ref, gain_ref = rest[:3]
    sems = rest[-1]
    copies = [
        pltpu.make_async_copy(far_qkv.at[pl.ds(1, 2)], qkv_ref, sems.at[0]),
        pltpu.make_async_copy(far_mod, mod_ref, sems.at[1]),
        pltpu.make_async_copy(far_gain, gain_ref, sems.at[2]),
    ]
    if marks:
        mark_ref = rest[3]
    for copy in copies:
        copy.start()
    if marks:
        place = lax.broadcasted_iota(jnp.int32, mark_ref.shape, 0)
        place = place + lax.axis_index("branch") * mark_ref.shape[0]
        mark_ref[...] = jnp.where(place < count_ref[0], 0.0, 1.0).astype(F32)
    for copy in copies:
        copy.wait()


def cut_kernel(n_head, near_ref, across_ref, far_qkv, *refs):
    pieces, query_ref, sem = refs[: n_head + 1], refs[n_head + 1], refs[n_head + 2]
    fetch = pltpu.make_async_copy(far_qkv.at[pl.ds(0, 1)], query_ref, sem)
    fetch.start()
    b = lax.axis_index("branch")
    h = lax.axis_index("head")
    per_core = n_head // 2
    part = pieces[0].shape[1]
    for k in range(n_head + 1):
        j = h ^ (k % n_head)
        half = b if k < n_head else 1 - b
        at = pl.ds(pl.multiple_of(lax.rem(j, per_core) * 2 * part + half * part, part), part)
        mine = lax.div(j, per_core) == b
        piece = pieces[k]

        @pl.when(mine)
        def _():
            piece[...] = near_ref[:, at]

        @pl.when(jnp.logical_not(mine))
        def _():
            piece[...] = across_ref[:, at]

    fetch.wait()


def contract(moded_ref, own_ref, other_ref, which, first, n_head):
    b = lax.axis_index("branch")
    h = lax.axis_index("head")
    quarter = moded_ref.shape[2]
    per_core = n_head // 2
    total = None
    for ref, core, at in ((own_ref, b, which - first), (other_ref, 1 - b, which)):
        for i in range(per_core):
            piece = moded_ref[(core * per_core + i) ^ h]
            term = jnp.dot(
                piece,
                ref[at, i * quarter : (i + 1) * quarter, :],
                preferred_element_type=F32,
            )
            total = term if total is None else total + term
    return total


def norm_heads(part, gain, width):
    outs = []
    for lo in range(0, width, HEAD_DIM):
        one = part[:, lo : lo + HEAD_DIM]
        scale = lax.rsqrt(jnp.mean(one * one, axis=1, keepdims=True) + EPS)
        outs.append(one * scale * gain)
    return outs


def kv_kernel(blk, chunk, n_head, *refs):
    xs = refs[:n_head]
    own_ref, other_ref, mod_ref, gain_ref, mark_ref, packed_ref, moded_ref = refs[n_head:]
    rows = xs[0].shape[0]
    padding = mark_ref[chunk * rows : (chunk + 1) * rows, :] > 0.5
    h = lax.axis_index("head")
    quarter = xs[0].shape[1]
    width = own_ref.shape[2]
    total = sum(jnp.sum(x[...].astype(F32), axis=1, keepdims=True) for x in xs)
    mean = total / (n_head * quarter)
    square = 0.0
    for x in xs:
        centered = x[...].astype(F32) - mean
        square = square + jnp.sum(centered * centered, axis=1, keepdims=True)
    scale = lax.rsqrt(square / (n_head * quarter) + EPS)
    for k, x in enumerate(xs):
        at = pl.ds(pl.multiple_of((h ^ k) * quarter, quarter), quarter)
        shift = mod_ref[0, blk : blk + 1, at]
        gain = mod_ref[1, blk : blk + 1, at] + 1.0
        normed = (x[...].astype(F32) - mean) * scale
        moded_ref[k] = (normed * gain + shift).astype(BF16)
    key = contract(moded_ref, own_ref, other_ref, 1, 1, n_head)
    for i, out in enumerate(norm_heads(key, gain_ref[blk, 1:2, :], width)):
        packed_ref[:, i * HEAD_DIM : (i + 1) * HEAD_DIM] = jnp.where(padding, MARK, out).astype(BF16)
    packed_ref[:, width:] = contract(moded_ref, own_ref, other_ref, 2, 1, n_head).astype(BF16)


def q_kernel(blk, n_head, chunks, *refs):
    moded = refs[:chunks]
    own_ref, other_ref, gain_ref, query_ref = refs[chunks:]
    width = own_ref.shape[2]
    rows = moded[0].shape[1]
    for c, moded_ref in enumerate(moded):
        query = contract(moded_ref, own_ref, other_ref, 0, 0, n_head)
        for i, out in enumerate(norm_heads(query, gain_ref[blk, 0:1, :], width)):
            query_ref[c * rows : (c + 1) * rows, i * HEAD_DIM : (i + 1) * HEAD_DIM] = out.astype(BF16)


def step_kernel(n, opens, closes, *refs):
    query_ref = refs[0]
    blocks = refs[1 : 1 + n]
    rest = refs[1 + n :]
    if not opens:
        mixed_in, stat_in, rest = rest[0], rest[1], rest[2:]
    width = query_ref.shape[1]
    scale = math.log2(math.e) / HEAD_DIM**0.5
    rows = query_ref.shape[0]
    ones = jnp.ones((16, HEAD_DIM), BF16)
    for i, lo in enumerate(range(0, width, HEAD_DIM)):
        at = slice(lo, lo + HEAD_DIM)
        key = jnp.concatenate([ref[:, at] for ref in blocks], axis=0)
        value = jnp.concatenate(
            [ref[:, width + lo : width + lo + HEAD_DIM] for ref in blocks], axis=0
        )
        query = jnp.concatenate([query_ref[:, at], ones], axis=0)
        scores = lax.dot_general(
            query, key, (((1,), (1,)), ((), ())), preferred_element_type=F32
        )
        drop = jnp.where(scores[rows : rows + 1, :] > MARK_SUM, -1e30, 0.0)
        scores = scores[:rows, :] * scale + drop
        peak = jnp.max(scores, axis=1, keepdims=True)
        if not opens:
            before = stat_in[0, :, i : i + 1]
            peak = jnp.maximum(peak, before)
        weight = jnp.exp2(scores - peak)
        total = jnp.sum(weight, axis=1, keepdims=True)
        mixed = jnp.dot(weight.astype(BF16), value, preferred_element_type=F32)
        if not opens:
            keep = jnp.exp2(before - peak)
            mixed = mixed + mixed_in[:, at] * keep
            total = total + stat_in[1, :, i : i + 1] * keep
        if closes:
            rest[0][:, at] = (mixed / total).astype(BF16)
        else:
            rest[0][:, at] = mixed
            rest[1][0, :, i : i + 1] = peak
            rest[1][1, :, i : i + 1] = total


def out_kernel(blk, n_head, chunks, closes, *refs):
    attended = refs[:n_head]
    mine = refs[n_head : 2 * n_head]
    others = refs[2 * n_head : 3 * n_head]
    xs = refs[3 * n_head : 3 * n_head + chunks]
    mod_ref = refs[3 * n_head + chunks]
    outs = refs[3 * n_head + chunks + 1 :]
    b = lax.axis_index("branch")
    h = lax.axis_index("head")
    rows, quarter = xs[0].shape
    part = mine[0].shape[1]
    for weights, core in ((mine, b), (others, 1 - b)):
        total = None
        for value, weight in zip(attended, weights):
            term = jnp.dot(value[...], weight[...], preferred_element_type=F32)
            total = term if total is None else total + term
        start = pl.multiple_of(core * part, part)
        at = pl.ds(pl.multiple_of(h * quarter + start, part), part)
        here = pl.ds(start, part)
        gate = mod_ref[2, blk : blk + 1, at]
        for c, x_ref in enumerate(xs):
            old = x_ref[:, here].astype(F32)
            own = slice(c * rows, (c + 1) * rows)
            new = (old + gate * total[own, :]).astype(BF16)
            if not closes:
                outs[c][:, here] = new
            else:
                outs[0][own, here] = new
                outs[1][own, here] = jnp.where(b == 0, x_ref[:, here], new)


def join_kernel(*refs):
    strong_ref, forked, got_ref, out_ref = refs[0], refs[1:-2], refs[-2], refs[-1]
    b = lax.axis_index("branch")
    rows = strong_ref.shape[0]
    each = forked[0].shape[0]

    @pl.when(b == 0)
    def _():
        out_ref[:rows, :] = strong_ref[...]
        out_ref[rows:, :] = got_ref[...]

    @pl.when(b != 0)
    def _():
        out_ref[:rows, :] = got_ref[...]
        for c, ref in enumerate(forked):
            out_ref[rows + c * each : rows + (c + 1) * each, :] = ref[...]


def groups_of(n_seq, chunks):
    ring = range(n_seq)
    parts = [[(c, core, i) for i in ring] for c in range(chunks) for core in range(2)]
    head = sum(parts[:-2], [])
    return ([head] if head else []) + parts[-2:]


def block(tokens, xs, valid, weights, outs, mod, gains, blk, sizes, later):
    n_branch, n_seq, n_head, chunks = sizes
    if blk == 0:
        weights = (weights, swap(weights))
        outs = (outs, swap(outs))
        xs = take_half(tokens, n_branch, chunks)
    rows, quarter = xs[0].shape
    full = rows * chunks
    width = weights[0].shape[2]
    part = quarter // n_branch
    pieces = [[x] + [cross(x, "head", k, n_head) for k in range(1, n_head)] for x in xs]
    marks = blk == 0
    qkv = weights[0]
    shape = [SHAPE((2,) + qkv.shape[1:], BF16), SHAPE(mod.shape, F32), SHAPE(gains.shape, F32)]
    shape += [SHAPE((full, HEAD_DIM), F32)] * marks
    own, near_mod, near_gains, *mark = pl.pallas_call(
        functools.partial(prep_kernel, marks),
        out_shape=shape,
        in_specs=[FAR] * 3 + [SMEM] * marks,
        out_specs=[VMEM] * (3 + marks),
        scratch_shapes=[pltpu.SemaphoreType.DMA((3,))],
        compiler_params=params(16),
    )(far(qkv), far(mod), far(gains), *([valid] * marks))
    valid = mark[0] if marks else valid
    weights = (own, weights[1])
    blocks, moded = [], []
    for c in range(chunks):
        packed, mods = pl.pallas_call(
            functools.partial(kv_kernel, blk, c, n_head),
            out_shape=(SHAPE((rows, 2 * width), BF16), SHAPE((n_head, rows, quarter), BF16)),
            in_specs=[VMEM] * (n_head + 5),
            out_specs=(VMEM, VMEM),
            compiler_params=params(16),
        )(*pieces[c], *weights, near_mod, near_gains, valid)
        moded.append(mods)
        blocks.append([packed] + [turn(packed, "seq", k, n_seq) for k in range(1, n_seq)])
    *spread, own = pl.pallas_call(
        functools.partial(cut_kernel, n_head),
        out_shape=[SHAPE((width, part), BF16)] * (n_head + 1)
        + [SHAPE((1,) + qkv.shape[1:], BF16)],
        in_specs=[VMEM] * 2 + [FAR],
        out_specs=[VMEM] * (n_head + 2),
        scratch_shapes=[pltpu.SemaphoreType.DMA],
        compiler_params=params(8),
    )(*outs, far(qkv))
    mine = [spread[0]] + [cross(spread[k], "head", k, n_head) for k in range(1, n_head)]
    query = pl.pallas_call(
        functools.partial(q_kernel, blk, n_head, chunks),
        out_shape=SHAPE((full, width), BF16),
        in_specs=[VMEM] * (chunks + 3),
        out_specs=VMEM,
        compiler_params=params(16),
    )(*moded, own, weights[1], near_gains)
    if blk == 0:
        qkv, out_weight = later
        later = ((qkv, swap(qkv)), (out_weight, swap(out_weight)))
    held = [[line, [swap(p) for p in line]] for line in blocks]
    others = [spread[n_head]] + [swap(p) for p in mine[1:]]
    groups = groups_of(n_seq, chunks)
    carry = []
    for i, group in enumerate(groups):
        closes = i == len(groups) - 1
        shape = [SHAPE((full, width), F32), SHAPE((2, full, HEAD_DIM), F32)]
        if closes:
            shape = [SHAPE((full, width), BF16)]
        carry = pl.pallas_call(
            functools.partial(step_kernel, len(group), i == 0, closes),
            out_shape=shape,
            in_specs=[VMEM] * (1 + len(group) + len(carry)),
            out_specs=[VMEM] * len(shape),
            compiler_params=params(16),
        )(query, *[held[c][core][k] for c, core, k in group], *carry)
    (attended,) = carry
    gathered = [attended] + [cross(attended, "head", k, n_head) for k in range(1, n_head)]
    shape = [SHAPE((rows, quarter), BF16)] * chunks
    if blk == 1:
        shape = [SHAPE((full, quarter), BF16)] * 2
    out = pl.pallas_call(
        functools.partial(out_kernel, blk, n_head, chunks, blk == 1),
        out_shape=shape,
        in_specs=[VMEM] * (3 * n_head + chunks + 1),
        out_specs=[VMEM] * len(shape),
        compiler_params=params(16),
    )(*gathered, *mine, *others, *xs, near_mod)
    return out, valid, later


def solution(mesh):
    n_branch, n_seq, n_head = (mesh.shape[a] for a in ("branch", "seq", "head"))
    chunks = 2 if n_seq <= 8 else 1
    sizes = n_branch, n_seq, n_head, chunks

    def per_device(
        tokens, valid_counts, shared_qkv, shared_out, skipped_qkv, skipped_out, modulation, qk_gains
    ):
        mod = modulation.transpose(1, 0, 2)
        later = skipped_qkv.transpose(1, 0, 2), skipped_out
        forked, valid, later = block(
            tokens, None, valid_counts, shared_qkv.transpose(1, 0, 2), shared_out, mod,
            qk_gains, 0, sizes, later,
        )
        (strong, sent), _, _ = block(
            None, forked, valid, *later, mod, qk_gains, 1, sizes, None
        )
        got = swap(sent)
        rows, quarter = strong.shape
        out = pl.pallas_call(
            join_kernel,
            out_shape=SHAPE((2 * rows, quarter), BF16),
            in_specs=[VMEM] * (2 + chunks),
            out_specs=VMEM,
            compiler_params=params(8),
            name="join",
        )(strong, *forked, got)
        return out[None]

    in_specs = (
        P("seq", "head"),
        P("seq"),
        P("branch", None, "head"),
        P("head", "branch"),
        P("branch", None, "head"),
        P("head", "branch"),
        P(),
        P(),
    )
    return jax.shard_map(
        per_device,
        mesh=mesh,
        in_specs=in_specs,
        out_specs=P("branch", "seq", "head"),
        check_vma=False,
    )
```

```python
import functools
import math

import jax
import jax.numpy as jnp
from jax import lax
from jax.experimental import pallas as pl
from jax.experimental.pallas import tpu as pltpu
from jax.sharding import PartitionSpec as P


HEAD_DIM = 128
EPS = 1e-06
MARK = 1e4
MARK_SUM = 1e5
F32 = jnp.float32
BF16 = jnp.bfloat16
VMEM = pl.BlockSpec(memory_space=pltpu.VMEM)
SMEM = pl.BlockSpec(memory_space=pltpu.SMEM)
FAR = pl.BlockSpec(memory_space=pl.ANY)
MIB = 1 << 20
SHAPE = jax.ShapeDtypeStruct


def turn(x, axis, k, n):
    return lax.ppermute(x, axis, [(i, (i + k) % n) for i in range(n)])


def cross(x, axis, k, n):
    return lax.ppermute(x, axis, [(i, i ^ k) for i in range(n)])


def swap(x):
    return lax.ppermute(x, "branch", [(0, 1), (1, 0)])


def far(x):
    return pltpu.with_memory_space_constraint(x, pltpu.HBM)


def params(mib):
    return pltpu.CompilerParams(vmem_limit_bytes=mib * MIB)


def half_kernel(tok_ref, *refs):
    outs, sem = refs[:-1], refs[-1]
    rows = outs[0].shape[0]
    start = pl.multiple_of(lax.axis_index("branch") * len(outs) * rows, rows)
    copies = [
        pltpu.make_async_copy(tok_ref.at[pl.ds(start + i * rows, rows)], out, sem.at[i])
        for i, out in enumerate(outs)
    ]
    for copy in copies:
        copy.start()
    for copy in copies:
        copy.wait()


def take_half(tokens, n_branch, chunks):
    rows, cols = tokens.shape
    return pl.pallas_call(
        half_kernel,
        out_shape=[SHAPE((rows // n_branch // chunks, cols), tokens.dtype)] * chunks,
        in_specs=[FAR],
        out_specs=[VMEM] * chunks,
        scratch_shapes=[pltpu.SemaphoreType.DMA((chunks,))],
        compiler_params=params(4),
        name="take_half",
    )(far(tokens))


def prep_kernel(far_qkv, far_mod, far_gain, count_ref, qkv_ref, mod_ref, gain_ref, mark_ref, sems):
    copies = [
        pltpu.make_async_copy(far_qkv.at[pl.ds(1, 2)], qkv_ref, sems.at[0]),
        pltpu.make_async_copy(far_mod, mod_ref, sems.at[1]),
        pltpu.make_async_copy(far_gain, gain_ref, sems.at[2]),
    ]
    for copy in copies:
        copy.start()
    place = lax.broadcasted_iota(jnp.int32, mark_ref.shape, 0)
    place = place + lax.axis_index("branch") * mark_ref.shape[0]
    mark_ref[...] = jnp.where(place < count_ref[0], 0.0, 1.0).astype(F32)
    for copy in copies:
        copy.wait()


def cut_kernel(n_head, near_ref, across_ref, *pieces):
    b = lax.axis_index("branch")
    h = lax.axis_index("head")
    per_core = n_head // 2
    part = pieces[0].shape[1]
    for k in range(n_head + 1):
        j = h ^ (k % n_head)
        half = b if k < n_head else 1 - b
        at = pl.ds(pl.multiple_of(lax.rem(j, per_core) * 2 * part + half * part, part), part)
        mine = lax.div(j, per_core) == b
        piece = pieces[k]

        @pl.when(mine)
        def _():
            piece[...] = near_ref[:, at]

        @pl.when(jnp.logical_not(mine))
        def _():
            piece[...] = across_ref[:, at]


def contract(moded_ref, own_ref, other_ref, which, first, n_head):
    b = lax.axis_index("branch")
    h = lax.axis_index("head")
    quarter = moded_ref.shape[2]
    per_core = n_head // 2
    total = None
    for ref, core, at in ((own_ref, b, which - first), (other_ref, 1 - b, which)):
        for i in range(per_core):
            piece = moded_ref[(core * per_core + i) ^ h]
            term = jnp.dot(
                piece,
                ref[at, i * quarter : (i + 1) * quarter, :],
                preferred_element_type=F32,
            )
            total = term if total is None else total + term
    return total


def norm_heads(part, gain, width):
    outs = []
    for lo in range(0, width, HEAD_DIM):
        one = part[:, lo : lo + HEAD_DIM]
        scale = lax.rsqrt(jnp.mean(one * one, axis=1, keepdims=True) + EPS)
        outs.append(one * scale * gain)
    return outs


def kv_kernel(blk, chunk, n_head, *refs):
    xs = refs[:n_head]
    own_ref, other_ref, mod_ref, gain_ref, mark_ref, packed_ref, moded_ref = refs[n_head:]
    rows = xs[0].shape[0]
    first = other_ref.shape[0] - own_ref.shape[0]
    padding = mark_ref[chunk * rows : (chunk + 1) * rows, :] > 0.5
    h = lax.axis_index("head")
    quarter = xs[0].shape[1]
    width = own_ref.shape[2]
    total = sum(jnp.sum(x[...].astype(F32), axis=1, keepdims=True) for x in xs)
    mean = total / (n_head * quarter)
    square = 0.0
    for x in xs:
        centered = x[...].astype(F32) - mean
        square = square + jnp.sum(centered * centered, axis=1, keepdims=True)
    scale = lax.rsqrt(square / (n_head * quarter) + EPS)
    for k, x in enumerate(xs):
        at = pl.ds(pl.multiple_of((h ^ k) * quarter, quarter), quarter)
        shift = mod_ref[0, blk : blk + 1, at]
        gain = mod_ref[1, blk : blk + 1, at] + 1.0
        normed = (x[...].astype(F32) - mean) * scale
        moded_ref[k] = (normed * gain + shift).astype(BF16)
    key = contract(moded_ref, own_ref, other_ref, 1, first, n_head)
    for i, out in enumerate(norm_heads(key, gain_ref[blk, 1:2, :], width)):
        packed_ref[:, i * HEAD_DIM : (i + 1) * HEAD_DIM] = jnp.where(padding, MARK, out).astype(BF16)
    packed_ref[:, width:] = contract(moded_ref, own_ref, other_ref, 2, first, n_head).astype(BF16)


def q_kernel(blk, n_head, chunks, *refs):
    moded = refs[:chunks]
    own_ref, other_ref, gain_ref, query_ref = refs[chunks:]
    width = own_ref.shape[2]
    rows = moded[0].shape[1]
    for c, moded_ref in enumerate(moded):
        query = contract(moded_ref, own_ref, other_ref, 0, 0, n_head)
        for i, out in enumerate(norm_heads(query, gain_ref[blk, 0:1, :], width)):
            query_ref[c * rows : (c + 1) * rows, i * HEAD_DIM : (i + 1) * HEAD_DIM] = out.astype(BF16)


def step_kernel(n, opens, closes, *refs):
    query_ref = refs[0]
    blocks = refs[1 : 1 + n]
    rest = refs[1 + n :]
    if not opens:
        mixed_in, stat_in, rest = rest[0], rest[1], rest[2:]
    width = query_ref.shape[1]
    scale = math.log2(math.e) / HEAD_DIM**0.5
    rows = query_ref.shape[0]
    ones = jnp.ones((16, HEAD_DIM), BF16)
    heads = [slice(lo, lo + HEAD_DIM) for lo in range(0, width, HEAD_DIM)]
    raw = []
    for at in heads:
        key = jnp.concatenate([ref[:, at] for ref in blocks], axis=0)
        query = jnp.concatenate([query_ref[:, at], ones], axis=0)
        raw.append(
            lax.dot_general(query, key, (((1,), (1,)), ((), ())), preferred_element_type=F32)
        )
    drop = jnp.where(raw[0][rows : rows + 1, :] > MARK_SUM, -1e30, 0.0)
    scores = [one[:rows, :] * scale + drop for one in raw]
    peaks = [jnp.max(one, axis=1, keepdims=True) for one in scores]
    if not opens:
        before = [stat_in[0, :, i : i + 1] for i in range(len(heads))]
        peaks = [jnp.maximum(one, old) for one, old in zip(peaks, before)]
    weights = [jnp.exp2(one - peak) for one, peak in zip(scores, peaks)]
    totals = [jnp.sum(one, axis=1, keepdims=True) for one in weights]
    for i, at in enumerate(heads):
        value = jnp.concatenate(
            [ref[:, width + at.start : width + at.stop] for ref in blocks], axis=0
        )
        mixed = jnp.dot(weights[i].astype(BF16), value, preferred_element_type=F32)
        total = totals[i]
        if not opens:
            keep = jnp.exp2(before[i] - peaks[i])
            mixed = mixed + mixed_in[:, at] * keep
            total = total + stat_in[1, :, i : i + 1] * keep
        if closes:
            rest[0][:, at] = (mixed / total).astype(BF16)
        else:
            rest[0][:, at] = mixed
            rest[1][0, :, i : i + 1] = peaks[i]
            rest[1][1, :, i : i + 1] = total


def out_kernel(blk, n_head, chunks, closes, *refs):
    attended = refs[:n_head]
    mine = refs[n_head : 2 * n_head]
    others = refs[2 * n_head : 3 * n_head]
    xs = refs[3 * n_head : 3 * n_head + chunks]
    mod_ref = refs[3 * n_head + chunks]
    outs = refs[3 * n_head + chunks + 1 :]
    b = lax.axis_index("branch")
    h = lax.axis_index("head")
    rows, quarter = xs[0].shape
    part = mine[0].shape[1]
    for weights, core in ((mine, b), (others, 1 - b)):
        total = None
        for value, weight in zip(attended, weights):
            term = jnp.dot(value[...], weight[...], preferred_element_type=F32)
            total = term if total is None else total + term
        start = pl.multiple_of(core * part, part)
        at = pl.ds(pl.multiple_of(h * quarter + start, part), part)
        here = pl.ds(start, part)
        gate = mod_ref[2, blk : blk + 1, at]
        for c, x_ref in enumerate(xs):
            old = x_ref[:, here].astype(F32)
            own = slice(c * rows, (c + 1) * rows)
            new = (old + gate * total[own, :]).astype(BF16)
            if not closes:
                outs[c][:, here] = new
            else:
                outs[0][own, here] = new
                outs[1][own, here] = jnp.where(b == 0, x_ref[:, here], new)


def join_kernel(*refs):
    strong_ref, forked, got_ref, out_ref = refs[0], refs[1:-2], refs[-2], refs[-1]
    b = lax.axis_index("branch")
    rows = strong_ref.shape[0]
    each = forked[0].shape[0]

    @pl.when(b == 0)
    def _():
        out_ref[:rows, :] = strong_ref[...]
        out_ref[rows:, :] = got_ref[...]

    @pl.when(b != 0)
    def _():
        out_ref[:rows, :] = got_ref[...]
        for c, ref in enumerate(forked):
            out_ref[rows + c * each : rows + (c + 1) * each, :] = ref[...]


def groups_of(n_seq, chunks):
    ring = range(n_seq)
    parts = [[(c, core, i) for i in ring] for c in range(chunks) for core in range(2)]
    joined = [parts[0]]
    for i in range(1, len(parts) - 1, 2):
        joined.append(parts[i] + parts[i + 1])
    return joined + parts[-1:]


def block(tokens, xs, valid, weights, outs, mod, gains, blk, sizes, later):
    n_branch, n_seq, n_head, chunks = sizes
    if blk == 0:
        weights = (weights, swap(weights))
        outs = (outs, swap(outs))
        xs = take_half(tokens, n_branch, chunks)
    rows, quarter = xs[0].shape
    full = rows * chunks
    width = weights[0].shape[2]
    part = quarter // n_branch
    pieces = [[x] + [cross(x, "head", k, n_head) for k in range(1, n_head)] for x in xs]
    qkv = weights[0]
    if blk == 0:
        shape = [SHAPE((2,) + qkv.shape[1:], BF16)]
        shape += [SHAPE(mod.shape, F32), SHAPE(gains.shape, F32), SHAPE((full, HEAD_DIM), F32)]
        own, mod, gains, valid = pl.pallas_call(
            prep_kernel,
            out_shape=shape,
            in_specs=[FAR] * 3 + [SMEM],
            out_specs=[VMEM] * 4,
            scratch_shapes=[pltpu.SemaphoreType.DMA((3,))],
            compiler_params=params(16),
            name="prep",
        )(far(qkv), far(mod), far(gains), valid)
    else:
        own = qkv
    blocks, moded = [], []
    for c in range(chunks):
        packed, mods = pl.pallas_call(
            functools.partial(kv_kernel, blk, c, n_head),
            out_shape=(SHAPE((rows, 2 * width), BF16), SHAPE((n_head, rows, quarter), BF16)),
            in_specs=[VMEM] * (n_head + 5),
            out_specs=(VMEM, VMEM),
            compiler_params=params(16),
        )(*pieces[c], own, weights[1], mod, gains, valid)
        moded.append(mods)
        blocks.append([packed] + [turn(packed, "seq", k, n_seq) for k in range(1, n_seq)])
    spread = pl.pallas_call(
        functools.partial(cut_kernel, n_head),
        out_shape=[SHAPE((width, part), BF16)] * (n_head + 1),
        in_specs=[VMEM] * 2,
        out_specs=[VMEM] * (n_head + 1),
        compiler_params=params(8),
    )(*outs)
    mine = [spread[0]] + [cross(spread[k], "head", k, n_head) for k in range(1, n_head)]
    query = pl.pallas_call(
        functools.partial(q_kernel, blk, n_head, chunks),
        out_shape=SHAPE((full, width), BF16),
        in_specs=[VMEM] * (chunks + 3),
        out_specs=VMEM,
        compiler_params=params(16),
    )(*moded, *weights, gains)
    if blk == 0:
        qkv, out_weight = later
        later = ((qkv, swap(qkv)), (out_weight, swap(out_weight)))
    held = [[line, [swap(p) for p in line]] for line in blocks]
    others = [spread[n_head]] + [swap(p) for p in mine[1:]]
    groups = groups_of(n_seq, chunks)
    carry = []
    for i, group in enumerate(groups):
        closes = i == len(groups) - 1
        shape = [SHAPE((full, width), F32), SHAPE((2, full, HEAD_DIM), F32)]
        if closes:
            shape = [SHAPE((full, width), BF16)]
        carry = pl.pallas_call(
            functools.partial(step_kernel, len(group), i == 0, closes),
            out_shape=shape,
            in_specs=[VMEM] * (1 + len(group) + len(carry)),
            out_specs=[VMEM] * len(shape),
            compiler_params=params(16),
        )(query, *[held[c][core][k] for c, core, k in group], *carry)
    (attended,) = carry
    gathered = [attended] + [cross(attended, "head", k, n_head) for k in range(1, n_head)]
    shape = [SHAPE((rows, quarter), BF16)] * chunks
    if blk == 1:
        shape = [SHAPE((full, quarter), BF16)] * 2
    out = pl.pallas_call(
        functools.partial(out_kernel, blk, n_head, chunks, blk == 1),
        out_shape=shape,
        in_specs=[VMEM] * (3 * n_head + chunks + 1),
        out_specs=[VMEM] * len(shape),
        compiler_params=params(16),
    )(*gathered, *mine, *others, *xs, mod)
    return out, (valid, mod, gains), later


def solution(mesh):
    n_branch, n_seq, n_head = (mesh.shape[a] for a in ("branch", "seq", "head"))
    chunks = 2 if n_seq <= 8 else 1
    sizes = n_branch, n_seq, n_head, chunks

    def per_device(
        tokens, valid_counts, shared_qkv, shared_out, skipped_qkv, skipped_out, modulation, qk_gains
    ):
        mod = modulation.transpose(1, 0, 2)
        later = skipped_qkv.transpose(1, 0, 2), skipped_out
        forked, near, later = block(
            tokens, None, valid_counts, shared_qkv.transpose(1, 0, 2), shared_out, mod,
            qk_gains, 0, sizes, later,
        )
        valid, mod, gains = near
        (strong, sent), _, _ = block(
            None, forked, valid, *later, mod, gains, 1, sizes, None
        )
        got = swap(sent)
        rows, quarter = strong.shape
        out = pl.pallas_call(
            join_kernel,
            out_shape=SHAPE((2 * rows, quarter), BF16),
            in_specs=[VMEM] * (2 + chunks),
            out_specs=VMEM,
            compiler_params=params(8),
            name="join",
        )(strong, *forked, got)
        return out[None]

    in_specs = (
        P("seq", "head"),
        P("seq"),
        P("branch", None, "head"),
        P("head", "branch"),
        P("branch", None, "head"),
        P("head", "branch"),
        P(),
        P(),
    )
    return jax.shard_map(
        per_device,
        mesh=mesh,
        in_specs=in_specs,
        out_specs=P("branch", "seq", "head"),
        check_vma=False,
    )
```

```python
import functools
import math

import jax
import jax.numpy as jnp
from jax import lax
from jax.experimental import pallas as pl
from jax.experimental.pallas import tpu as pltpu
from jax.sharding import PartitionSpec as P


HEAD_DIM = 128
EPS = 1e-06
MARK = 1e4
MARK_SUM = 1e5
F32 = jnp.float32
BF16 = jnp.bfloat16
VMEM = pl.BlockSpec(memory_space=pltpu.VMEM)
SMEM = pl.BlockSpec(memory_space=pltpu.SMEM)
FAR = pl.BlockSpec(memory_space=pl.ANY)
MIB = 1 << 20
SHAPE = jax.ShapeDtypeStruct


def turn(x, axis, k, n):
    return lax.ppermute(x, axis, [(i, (i + k) % n) for i in range(n)])


def cross(x, axis, k, n):
    return lax.ppermute(x, axis, [(i, i ^ k) for i in range(n)])


def swap(x):
    return lax.ppermute(x, "branch", [(0, 1), (1, 0)])


def far(x):
    return pltpu.with_memory_space_constraint(x, pltpu.HBM)


def params(mib):
    return pltpu.CompilerParams(vmem_limit_bytes=mib * MIB)


def half_kernel(tok_ref, *refs):
    outs, sem = refs[:-1], refs[-1]
    rows = outs[0].shape[0]
    start = pl.multiple_of(lax.axis_index("branch") * len(outs) * rows, rows)
    copies = [
        pltpu.make_async_copy(tok_ref.at[pl.ds(start + i * rows, rows)], out, sem.at[i])
        for i, out in enumerate(outs)
    ]
    for copy in copies:
        copy.start()
    for copy in copies:
        copy.wait()


def take_half(tokens, n_branch, chunks):
    rows, cols = tokens.shape
    return pl.pallas_call(
        half_kernel,
        out_shape=[SHAPE((rows // n_branch // chunks, cols), tokens.dtype)] * chunks,
        in_specs=[FAR],
        out_specs=[VMEM] * chunks,
        scratch_shapes=[pltpu.SemaphoreType.DMA((chunks,))],
        compiler_params=params(4),
        name="take_half",
    )(far(tokens))


def prep_kernel(far_qkv, far_mod, far_gain, count_ref, qkv_ref, mod_ref, gain_ref, mark_ref, sems):
    depth = qkv_ref.shape[1] // 4
    copies = [
        pltpu.make_async_copy(
            far_qkv.at[i + 1, pl.ds(j * depth, depth)],
            qkv_ref.at[i, pl.ds(j * depth, depth)],
            sems.at[i * 4 + j],
        )
        for i in range(2)
        for j in range(4)
    ]
    copies += [
        pltpu.make_async_copy(far_mod, mod_ref, sems.at[8]),
        pltpu.make_async_copy(far_gain, gain_ref, sems.at[9]),
    ]
    for copy in copies:
        copy.start()
    place = lax.broadcasted_iota(jnp.int32, mark_ref.shape, 0)
    place = place + lax.axis_index("branch") * mark_ref.shape[0]
    mark_ref[...] = jnp.where(place < count_ref[0], 0.0, 1.0).astype(F32)
    for copy in copies:
        copy.wait()


def cut_kernel(n_head, near_ref, across_ref, *pieces):
    b = lax.axis_index("branch")
    h = lax.axis_index("head")
    per_core = n_head // 2
    part = pieces[0].shape[1]
    for k in range(n_head + 1):
        j = h ^ (k % n_head)
        half = b if k < n_head else 1 - b
        at = pl.ds(pl.multiple_of(lax.rem(j, per_core) * 2 * part + half * part, part), part)
        mine = lax.div(j, per_core) == b
        piece = pieces[k]

        @pl.when(mine)
        def _():
            piece[...] = near_ref[:, at]

        @pl.when(jnp.logical_not(mine))
        def _():
            piece[...] = across_ref[:, at]


def contract(moded, own_ref, other_ref, which, first, n_head):
    b = lax.axis_index("branch")
    h = lax.axis_index("head")
    quarter = moded[0].shape[2]
    per_core = n_head // 2
    total = None
    for ref, core, at in ((own_ref, b, which - first), (other_ref, 1 - b, which)):
        for i in range(per_core):
            piece = jnp.concatenate([m[(core * per_core + i) ^ h] for m in moded], axis=0)
            term = jnp.dot(
                piece,
                ref[at, i * quarter : (i + 1) * quarter, :],
                preferred_element_type=F32,
            )
            total = term if total is None else total + term
    return total


def norm_heads(part, gain, width):
    outs = []
    for lo in range(0, width, HEAD_DIM):
        one = part[:, lo : lo + HEAD_DIM]
        scale = lax.rsqrt(jnp.mean(one * one, axis=1, keepdims=True) + EPS)
        outs.append(one * scale * gain)
    return outs


def kv_kernel(blk, chunk, n_head, *refs):
    xs = refs[:n_head]
    own_ref, other_ref, mod_ref, gain_ref, mark_ref, packed_ref, moded_ref = refs[n_head:]
    rows = xs[0].shape[0]
    first = other_ref.shape[0] - own_ref.shape[0]
    padding = mark_ref[chunk * rows : (chunk + 1) * rows, :] > 0.5
    h = lax.axis_index("head")
    quarter = xs[0].shape[1]
    width = own_ref.shape[2]
    total = sum(jnp.sum(x[...].astype(F32), axis=1, keepdims=True) for x in xs)
    mean = total / (n_head * quarter)
    square = 0.0
    for x in xs:
        centered = x[...].astype(F32) - mean
        square = square + jnp.sum(centered * centered, axis=1, keepdims=True)
    scale = lax.rsqrt(square / (n_head * quarter) + EPS)
    for k, x in enumerate(xs):
        at = pl.ds(pl.multiple_of((h ^ k) * quarter, quarter), quarter)
        shift = mod_ref[0, blk : blk + 1, at]
        gain = mod_ref[1, blk : blk + 1, at] + 1.0
        normed = (x[...].astype(F32) - mean) * scale
        moded_ref[k] = (normed * gain + shift).astype(BF16)
    key = contract([moded_ref], own_ref, other_ref, 1, first, n_head)
    for i, out in enumerate(norm_heads(key, gain_ref[blk, 1:2, :], width)):
        packed_ref[:, i * HEAD_DIM : (i + 1) * HEAD_DIM] = jnp.where(padding, MARK, out).astype(BF16)
    packed_ref[:, width:] = contract([moded_ref], own_ref, other_ref, 2, first, n_head).astype(BF16)


def q_kernel(blk, n_head, chunks, *refs):
    moded = refs[:chunks]
    own_ref, other_ref, gain_ref, query_ref = refs[chunks:]
    width = own_ref.shape[2]
    query = contract(moded, own_ref, other_ref, 0, 0, n_head)
    for i, out in enumerate(norm_heads(query, gain_ref[blk, 0:1, :], width)):
        query_ref[:, i * HEAD_DIM : (i + 1) * HEAD_DIM] = out.astype(BF16)


def step_kernel(n, opens, closes, *refs):
    query_ref = refs[0]
    blocks = refs[1 : 1 + n]
    rest = refs[1 + n :]
    if not opens:
        mixed_in, stat_in, rest = rest[0], rest[1], rest[2:]
    width = query_ref.shape[1]
    scale = math.log2(math.e) / HEAD_DIM**0.5
    rows = query_ref.shape[0]
    ones = jnp.ones((16, HEAD_DIM), BF16)
    heads = [slice(lo, lo + HEAD_DIM) for lo in range(0, width, HEAD_DIM)]
    raw = []
    for at in heads:
        key = jnp.concatenate([ref[:, at] for ref in blocks], axis=0)
        query = jnp.concatenate([query_ref[:, at], ones], axis=0)
        raw.append(
            lax.dot_general(query, key, (((1,), (1,)), ((), ())), preferred_element_type=F32)
        )
    drop = jnp.where(raw[0][rows : rows + 1, :] > MARK_SUM, -1e30, 0.0)
    scores = [one[:rows, :] * scale + drop for one in raw]
    peaks = [jnp.max(one, axis=1, keepdims=True) for one in scores]
    if not opens:
        before = [stat_in[0, :, i : i + 1] for i in range(len(heads))]
        peaks = [jnp.maximum(one, old) for one, old in zip(peaks, before)]
    weights = [jnp.exp2(one - peak) for one, peak in zip(scores, peaks)]
    totals = [jnp.sum(one, axis=1, keepdims=True) for one in weights]
    for i, at in enumerate(heads):
        value = jnp.concatenate(
            [ref[:, width + at.start : width + at.stop] for ref in blocks], axis=0
        )
        mixed = jnp.dot(weights[i].astype(BF16), value, preferred_element_type=F32)
        total = totals[i]
        if not opens:
            keep = jnp.exp2(before[i] - peaks[i])
            mixed = mixed + mixed_in[:, at] * keep
            total = total + stat_in[1, :, i : i + 1] * keep
        if closes:
            rest[0][:, at] = (mixed / total).astype(BF16)
        else:
            rest[0][:, at] = mixed
            rest[1][0, :, i : i + 1] = peaks[i]
            rest[1][1, :, i : i + 1] = total


def out_kernel(blk, n_head, chunks, closes, *refs):
    attended = refs[:n_head]
    mine = refs[n_head : 2 * n_head]
    others = refs[2 * n_head : 3 * n_head]
    xs = refs[3 * n_head : 3 * n_head + chunks]
    mod_ref = refs[3 * n_head + chunks]
    outs = refs[3 * n_head + chunks + 1 :]
    b = lax.axis_index("branch")
    h = lax.axis_index("head")
    rows, quarter = xs[0].shape
    part = mine[0].shape[1]
    for weights, core in ((mine, b), (others, 1 - b)):
        total = None
        for value, weight in zip(attended, weights):
            term = jnp.dot(value[...], weight[...], preferred_element_type=F32)
            total = term if total is None else total + term
        start = pl.multiple_of(core * part, part)
        at = pl.ds(pl.multiple_of(h * quarter + start, part), part)
        here = pl.ds(start, part)
        gate = mod_ref[2, blk : blk + 1, at]
        for c, x_ref in enumerate(xs):
            old = x_ref[:, here].astype(F32)
            own = slice(c * rows, (c + 1) * rows)
            new = (old + gate * total[own, :]).astype(BF16)
            if not closes:
                outs[c][:, here] = new
            else:
                outs[0][own, here] = new
                outs[1][own, here] = jnp.where(b == 0, x_ref[:, here], new)


def join_kernel(*refs):
    strong_ref, forked, got_ref, out_ref = refs[0], refs[1:-2], refs[-2], refs[-1]
    b = lax.axis_index("branch")
    rows = strong_ref.shape[0]
    each = forked[0].shape[0]

    @pl.when(b == 0)
    def _():
        out_ref[:rows, :] = strong_ref[...]
        out_ref[rows:, :] = got_ref[...]

    @pl.when(b != 0)
    def _():
        out_ref[:rows, :] = got_ref[...]
        for c, ref in enumerate(forked):
            out_ref[rows + c * each : rows + (c + 1) * each, :] = ref[...]


def groups_of(n_seq, chunks):
    ring = range(n_seq)
    parts = [[(c, core, i) for i in ring] for c in range(chunks) for core in range(2)]
    joined = [parts[0]]
    for i in range(1, len(parts) - 1, 2):
        joined.append(parts[i] + parts[i + 1])
    return joined + parts[-1:]


def block(tokens, xs, valid, weights, outs, mod, gains, blk, sizes, later):
    n_branch, n_seq, n_head, chunks = sizes
    if blk == 0:
        weights = (weights, swap(weights))
        outs = (outs, swap(outs))
        xs = take_half(tokens, n_branch, chunks)
    rows, quarter = xs[0].shape
    full = rows * chunks
    width = weights[0].shape[2]
    part = quarter // n_branch
    pieces = [[x] + [cross(x, "head", k, n_head) for k in range(1, n_head)] for x in xs]
    qkv = weights[0]
    if blk == 0:
        shape = [SHAPE((2,) + qkv.shape[1:], BF16)]
        shape += [SHAPE(mod.shape, F32), SHAPE(gains.shape, F32), SHAPE((full, HEAD_DIM), F32)]
        own, mod, gains, valid = pl.pallas_call(
            prep_kernel,
            out_shape=shape,
            in_specs=[FAR] * 3 + [SMEM],
            out_specs=[VMEM] * 4,
            scratch_shapes=[pltpu.SemaphoreType.DMA((10,))],
            compiler_params=params(16),
            name="prep",
        )(far(qkv), far(mod), far(gains), valid)
    else:
        own = qkv
    blocks, moded = [], []
    for c in range(chunks):
        packed, mods = pl.pallas_call(
            functools.partial(kv_kernel, blk, c, n_head),
            out_shape=(SHAPE((rows, 2 * width), BF16), SHAPE((n_head, rows, quarter), BF16)),
            in_specs=[VMEM] * (n_head + 5),
            out_specs=(VMEM, VMEM),
            compiler_params=params(16),
        )(*pieces[c], own, weights[1], mod, gains, valid)
        moded.append(mods)
        blocks.append([packed] + [turn(packed, "seq", k, n_seq) for k in range(1, n_seq)])
    spread = pl.pallas_call(
        functools.partial(cut_kernel, n_head),
        out_shape=[SHAPE((width, part), BF16)] * (n_head + 1),
        in_specs=[VMEM] * 2,
        out_specs=[VMEM] * (n_head + 1),
        compiler_params=params(8),
    )(*outs)
    mine = [spread[0]] + [cross(spread[k], "head", k, n_head) for k in range(1, n_head)]
    query = pl.pallas_call(
        functools.partial(q_kernel, blk, n_head, chunks),
        out_shape=SHAPE((full, width), BF16),
        in_specs=[VMEM] * (chunks + 3),
        out_specs=VMEM,
        compiler_params=params(16),
    )(*moded, *weights, gains)
    if blk == 0:
        qkv, out_weight = later
        later = ((qkv, swap(qkv)), (out_weight, swap(out_weight)))
    held = [[line, [swap(p) for p in line]] for line in blocks]
    others = [spread[n_head]] + [swap(p) for p in mine[1:]]
    groups = groups_of(n_seq, chunks)
    carry = []
    for i, group in enumerate(groups):
        closes = i == len(groups) - 1
        shape = [SHAPE((full, width), F32), SHAPE((2, full, HEAD_DIM), F32)]
        if closes:
            shape = [SHAPE((full, width), BF16)]
        carry = pl.pallas_call(
            functools.partial(step_kernel, len(group), i == 0, closes),
            out_shape=shape,
            in_specs=[VMEM] * (1 + len(group) + len(carry)),
            out_specs=[VMEM] * len(shape),
            compiler_params=params(16),
        )(query, *[held[c][core][k] for c, core, k in group], *carry)
    (attended,) = carry
    gathered = [attended] + [cross(attended, "head", k, n_head) for k in range(1, n_head)]
    shape = [SHAPE((rows, quarter), BF16)] * chunks
    if blk == 1:
        shape = [SHAPE((full, quarter), BF16)] * 2
    out = pl.pallas_call(
        functools.partial(out_kernel, blk, n_head, chunks, blk == 1),
        out_shape=shape,
        in_specs=[VMEM] * (3 * n_head + chunks + 1),
        out_specs=[VMEM] * len(shape),
        compiler_params=params(16),
    )(*gathered, *mine, *others, *xs, mod)
    return out, (valid, mod, gains), later


def solution(mesh):
    n_branch, n_seq, n_head = (mesh.shape[a] for a in ("branch", "seq", "head"))
    chunks = 2 if n_seq <= 8 else 1
    sizes = n_branch, n_seq, n_head, chunks

    def per_device(
        tokens, valid_counts, shared_qkv, shared_out, skipped_qkv, skipped_out, modulation, qk_gains
    ):
        mod = modulation.transpose(1, 0, 2)
        later = skipped_qkv.transpose(1, 0, 2), skipped_out
        forked, near, later = block(
            tokens, None, valid_counts, shared_qkv.transpose(1, 0, 2), shared_out, mod,
            qk_gains, 0, sizes, later,
        )
        valid, mod, gains = near
        (strong, sent), _, _ = block(
            None, forked, valid, *later, mod, gains, 1, sizes, None
        )
        got = swap(sent)
        rows, quarter = strong.shape
        out = pl.pallas_call(
            join_kernel,
            out_shape=SHAPE((2 * rows, quarter), BF16),
            in_specs=[VMEM] * (2 + chunks),
            out_specs=VMEM,
            compiler_params=params(8),
            name="join",
        )(strong, *forked, got)
        return out[None]

    in_specs = (
        P("seq", "head"),
        P("seq"),
        P("branch", None, "head"),
        P("head", "branch"),
        P("branch", None, "head"),
        P("head", "branch"),
        P(),
        P(),
    )
    return jax.shard_map(
        per_device,
        mesh=mesh,
        in_specs=in_specs,
        out_specs=P("branch", "seq", "head"),
        check_vma=False,
    )
```

```python
import functools
import math

import jax
import jax.numpy as jnp
from jax import lax
from jax.experimental import pallas as pl
from jax.experimental.pallas import tpu as pltpu
from jax.sharding import PartitionSpec as P


HEAD_DIM = 128
EPS = 1e-06
MARK = 1e4
MARK_SUM = 1e5
F32 = jnp.float32
BF16 = jnp.bfloat16
VMEM = pl.BlockSpec(memory_space=pltpu.VMEM)
SMEM = pl.BlockSpec(memory_space=pltpu.SMEM)
FAR = pl.BlockSpec(memory_space=pl.ANY)
MIB = 1 << 20
SHAPE = jax.ShapeDtypeStruct


def turn(x, axis, k, n):
    return lax.ppermute(x, axis, [(i, (i + k) % n) for i in range(n)])


def cross(x, axis, k, n):
    return lax.ppermute(x, axis, [(i, i ^ k) for i in range(n)])


def swap(x):
    return lax.ppermute(x, "branch", [(0, 1), (1, 0)])


def far(x):
    return pltpu.with_memory_space_constraint(x, pltpu.HBM)


def params(mib):
    return pltpu.CompilerParams(vmem_limit_bytes=mib * MIB)


def half_kernel(tok_ref, *refs):
    outs, sem = refs[:-1], refs[-1]
    rows = outs[0].shape[0]
    start = pl.multiple_of(lax.axis_index("branch") * len(outs) * rows, rows)
    copies = [
        pltpu.make_async_copy(tok_ref.at[pl.ds(start + i * rows, rows)], out, sem.at[i])
        for i, out in enumerate(outs)
    ]
    for copy in copies:
        copy.start()
    for copy in copies:
        copy.wait()


def take_half(tokens, n_branch, chunks):
    rows, cols = tokens.shape
    return pl.pallas_call(
        half_kernel,
        out_shape=[SHAPE((rows // n_branch // chunks, cols), tokens.dtype)] * chunks,
        in_specs=[FAR],
        out_specs=[VMEM] * chunks,
        scratch_shapes=[pltpu.SemaphoreType.DMA((chunks,))],
        compiler_params=params(4),
        name="take_half",
    )(far(tokens))


def prep_kernel(far_qkv, far_mod, far_gain, count_ref, qkv_ref, mod_ref, gain_ref, mark_ref, sems):
    depth = qkv_ref.shape[1] // 4
    copies = [
        pltpu.make_async_copy(
            far_qkv.at[i + 1, pl.ds(j * depth, depth)],
            qkv_ref.at[i, pl.ds(j * depth, depth)],
            sems.at[i * 4 + j],
        )
        for i in range(2)
        for j in range(4)
    ]
    copies += [
        pltpu.make_async_copy(far_mod, mod_ref, sems.at[8]),
        pltpu.make_async_copy(far_gain, gain_ref, sems.at[9]),
    ]
    for copy in copies:
        copy.start()
    place = lax.broadcasted_iota(jnp.int32, mark_ref.shape, 0)
    place = place + lax.axis_index("branch") * mark_ref.shape[0]
    mark_ref[...] = jnp.where(place < count_ref[0], 0.0, 1.0).astype(F32)
    for copy in copies:
        copy.wait()


def cut_kernel(n_head, near_ref, across_ref, *pieces):
    b = lax.axis_index("branch")
    h = lax.axis_index("head")
    per_core = n_head // 2
    part = pieces[0].shape[1]
    for k in range(n_head + 1):
        j = h ^ (k % n_head)
        half = b if k < n_head else 1 - b
        at = pl.ds(pl.multiple_of(lax.rem(j, per_core) * 2 * part + half * part, part), part)
        mine = lax.div(j, per_core) == b
        piece = pieces[k]

        @pl.when(mine)
        def _():
            piece[...] = near_ref[:, at]

        @pl.when(jnp.logical_not(mine))
        def _():
            piece[...] = across_ref[:, at]


def contract(moded, own_ref, other_ref, which, first, n_head):
    b = lax.axis_index("branch")
    h = lax.axis_index("head")
    quarter = moded[0].shape[2]
    per_core = n_head // 2
    total = None
    for ref, core, at in ((own_ref, b, which - first), (other_ref, 1 - b, which)):
        for i in range(per_core):
            piece = jnp.concatenate([m[(core * per_core + i) ^ h] for m in moded], axis=0)
            term = jnp.dot(
                piece,
                ref[at, i * quarter : (i + 1) * quarter, :],
                preferred_element_type=F32,
            )
            total = term if total is None else total + term
    return total


def norm_heads(part, gain, width):
    outs = []
    for lo in range(0, width, HEAD_DIM):
        one = part[:, lo : lo + HEAD_DIM]
        scale = lax.rsqrt(jnp.mean(one * one, axis=1, keepdims=True) + EPS)
        outs.append(one * scale * gain)
    return outs


def kv_kernel(blk, chunk, n_head, *refs):
    xs = refs[:n_head]
    own_ref, other_ref, mod_ref, gain_ref, mark_ref, packed_ref, moded_ref = refs[n_head:]
    rows = xs[0].shape[0]
    first = other_ref.shape[0] - own_ref.shape[0]
    padding = mark_ref[chunk * rows : (chunk + 1) * rows, :] > 0.5
    h = lax.axis_index("head")
    quarter = xs[0].shape[1]
    width = own_ref.shape[2]
    total = sum(jnp.sum(x[...].astype(F32), axis=1, keepdims=True) for x in xs)
    mean = total / (n_head * quarter)
    square = 0.0
    for x in xs:
        centered = x[...].astype(F32) - mean
        square = square + jnp.sum(centered * centered, axis=1, keepdims=True)
    scale = lax.rsqrt(square / (n_head * quarter) + EPS)
    for k, x in enumerate(xs):
        at = pl.ds(pl.multiple_of((h ^ k) * quarter, quarter), quarter)
        shift = mod_ref[0, blk : blk + 1, at]
        gain = mod_ref[1, blk : blk + 1, at] + 1.0
        normed = (x[...].astype(F32) - mean) * scale
        moded_ref[k] = (normed * gain + shift).astype(BF16)
    key = contract([moded_ref], own_ref, other_ref, 1, first, n_head)
    for i, out in enumerate(norm_heads(key, gain_ref[blk, 1:2, :], width)):
        packed_ref[:, i * HEAD_DIM : (i + 1) * HEAD_DIM] = jnp.where(padding, MARK, out).astype(BF16)
    packed_ref[:, width:] = contract([moded_ref], own_ref, other_ref, 2, first, n_head).astype(BF16)


def q_kernel(blk, n_head, chunks, *refs):
    moded = refs[:chunks]
    own_ref, other_ref, gain_ref, query_ref = refs[chunks:]
    width = own_ref.shape[2]
    query = contract(moded, own_ref, other_ref, 0, 0, n_head)
    for i, out in enumerate(norm_heads(query, gain_ref[blk, 0:1, :], width)):
        query_ref[:, i * HEAD_DIM : (i + 1) * HEAD_DIM] = out.astype(BF16)


def step_kernel(n, opens, closes, *refs):
    query_ref = refs[0]
    blocks = refs[1 : 1 + n]
    rest = refs[1 + n :]
    if not opens:
        mixed_in, stat_in, rest = rest[0], rest[1], rest[2:]
    width = query_ref.shape[1]
    scale = math.log2(math.e) / HEAD_DIM**0.5
    rows = query_ref.shape[0]
    ones = jnp.ones((16, HEAD_DIM), BF16)
    if opens and len(rest) == 3:
        at = 0
        for ref in blocks:
            rest[2][at : at + ref.shape[0], :] = ref[...]
            at += ref.shape[0]
    heads = [slice(lo, lo + HEAD_DIM) for lo in range(0, width, HEAD_DIM)]
    raw = []
    for at in heads:
        key = jnp.concatenate([ref[:, at] for ref in blocks], axis=0)
        query = jnp.concatenate([query_ref[:, at], ones], axis=0)
        raw.append(
            lax.dot_general(query, key, (((1,), (1,)), ((), ())), preferred_element_type=F32)
        )
    drop = jnp.where(raw[0][rows : rows + 1, :] > MARK_SUM, -1e30, 0.0)
    scores = [one[:rows, :] * scale + drop for one in raw]
    peaks = [jnp.max(one, axis=1, keepdims=True) for one in scores]
    if not opens:
        before = [stat_in[0, :, i : i + 1] for i in range(len(heads))]
        peaks = [jnp.maximum(one, old) for one, old in zip(peaks, before)]
    weights = [jnp.exp2(one - peak) for one, peak in zip(scores, peaks)]
    totals = [jnp.sum(one, axis=1, keepdims=True) for one in weights]
    for i, at in enumerate(heads):
        value = jnp.concatenate(
            [ref[:, width + at.start : width + at.stop] for ref in blocks], axis=0
        )
        mixed = jnp.dot(weights[i].astype(BF16), value, preferred_element_type=F32)
        total = totals[i]
        if not opens:
            keep = jnp.exp2(before[i] - peaks[i])
            mixed = mixed + mixed_in[:, at] * keep
            total = total + stat_in[1, :, i : i + 1] * keep
        if closes:
            rest[0][:, at] = (mixed / total).astype(BF16)
        else:
            rest[0][:, at] = mixed
            rest[1][0, :, i : i + 1] = peaks[i]
            rest[1][1, :, i : i + 1] = total


def out_kernel(blk, n_head, chunks, closes, *refs):
    attended = refs[:n_head]
    mine = refs[n_head : 2 * n_head]
    others = refs[2 * n_head : 3 * n_head]
    xs = refs[3 * n_head : 3 * n_head + chunks]
    mod_ref = refs[3 * n_head + chunks]
    outs = refs[3 * n_head + chunks + 1 :]
    b = lax.axis_index("branch")
    h = lax.axis_index("head")
    rows, quarter = xs[0].shape
    part = mine[0].shape[1]
    for weights, core in ((mine, b), (others, 1 - b)):
        total = None
        for value, weight in zip(attended, weights):
            term = jnp.dot(value[...], weight[...], preferred_element_type=F32)
            total = term if total is None else total + term
        start = pl.multiple_of(core * part, part)
        at = pl.ds(pl.multiple_of(h * quarter + start, part), part)
        here = pl.ds(start, part)
        gate = mod_ref[2, blk : blk + 1, at]
        for c, x_ref in enumerate(xs):
            old = x_ref[:, here].astype(F32)
            own = slice(c * rows, (c + 1) * rows)
            new = (old + gate * total[own, :]).astype(BF16)
            if not closes:
                outs[c][:, here] = new
            else:
                outs[0][own, here] = new
                outs[1][own, here] = jnp.where(b == 0, x_ref[:, here], new)


def join_kernel(*refs):
    strong_ref, forked, got_ref, out_ref = refs[0], refs[1:-2], refs[-2], refs[-1]
    b = lax.axis_index("branch")
    rows = strong_ref.shape[0]
    each = forked[0].shape[0]

    @pl.when(b == 0)
    def _():
        out_ref[:rows, :] = strong_ref[...]
        out_ref[rows:, :] = got_ref[...]

    @pl.when(b != 0)
    def _():
        out_ref[:rows, :] = got_ref[...]
        for c, ref in enumerate(forked):
            out_ref[rows + c * each : rows + (c + 1) * each, :] = ref[...]


def groups_of(n_seq, chunks):
    ring = range(n_seq)
    parts = [[(c, core, i) for i in ring] for c in range(chunks) for core in range(2)]
    joined = [parts[0]]
    for i in range(1, len(parts) - 1, 2):
        joined.append(parts[i] + parts[i + 1])
    return joined + parts[-1:]


def block(tokens, xs, valid, weights, outs, mod, gains, blk, sizes, later):
    n_branch, n_seq, n_head, chunks = sizes
    if blk == 0:
        weights = (weights, swap(weights))
        outs = (outs, swap(outs))
        xs = take_half(tokens, n_branch, chunks)
    rows, quarter = xs[0].shape
    full = rows * chunks
    width = weights[0].shape[2]
    part = quarter // n_branch
    pieces = [[x] + [cross(x, "head", k, n_head) for k in range(1, n_head)] for x in xs]
    qkv = weights[0]
    if blk == 0:
        shape = [SHAPE((2,) + qkv.shape[1:], BF16)]
        shape += [SHAPE(mod.shape, F32), SHAPE(gains.shape, F32), SHAPE((full, HEAD_DIM), F32)]
        own, mod, gains, valid = pl.pallas_call(
            prep_kernel,
            out_shape=shape,
            in_specs=[FAR] * 3 + [SMEM],
            out_specs=[VMEM] * 4,
            scratch_shapes=[pltpu.SemaphoreType.DMA((10,))],
            compiler_params=params(16),
            name="prep",
        )(far(qkv), far(mod), far(gains), valid)
    else:
        own = qkv
    blocks, moded = [], []
    for c in range(chunks):
        packed, mods = pl.pallas_call(
            functools.partial(kv_kernel, blk, c, n_head),
            out_shape=(SHAPE((rows, 2 * width), BF16), SHAPE((n_head, rows, quarter), BF16)),
            in_specs=[VMEM] * (n_head + 5),
            out_specs=(VMEM, VMEM),
            compiler_params=params(16),
        )(*pieces[c], own, weights[1], mod, gains, valid)
        moded.append(mods)
        blocks.append([packed] + [turn(packed, "seq", k, n_seq) for k in range(1, n_seq)])
    spread = pl.pallas_call(
        functools.partial(cut_kernel, n_head),
        out_shape=[SHAPE((width, part), BF16)] * (n_head + 1),
        in_specs=[VMEM] * 2,
        out_specs=[VMEM] * (n_head + 1),
        compiler_params=params(8),
    )(*outs)
    mine = [spread[0]] + [cross(spread[k], "head", k, n_head) for k in range(1, n_head)]
    query = pl.pallas_call(
        functools.partial(q_kernel, blk, n_head, chunks),
        out_shape=SHAPE((full, width), BF16),
        in_specs=[VMEM] * (chunks + 3),
        out_specs=VMEM,
        compiler_params=params(16),
    )(*moded, *weights, gains)
    if blk == 0:
        qkv, out_weight = later
        later = ((qkv, swap(qkv)), (out_weight, swap(out_weight)))
    whole = chunks > 1
    held = [
        [line, [] if whole and c == 0 else [swap(p) for p in line]]
        for c, line in enumerate(blocks)
    ]
    others = [spread[n_head]] + [swap(p) for p in mine[1:]]
    groups = groups_of(n_seq, chunks)
    carry = []
    for i, group in enumerate(groups):
        closes = i == len(groups) - 1
        shape = [SHAPE((full, width), F32), SHAPE((2, full, HEAD_DIM), F32)]
        if closes:
            shape = [SHAPE((full, width), BF16)]
        elif whole and i == 0:
            shape.append(SHAPE((len(group) * rows, 2 * width), BF16))
        taken = [held[c][core][k] for c, core, k in group if held[c][core]]
        if whole and i == 1:
            taken = [swap(pack)] + taken
        carry = pl.pallas_call(
            functools.partial(step_kernel, len(taken), i == 0, closes),
            out_shape=shape,
            in_specs=[VMEM] * (1 + len(taken) + len(carry)),
            out_specs=[VMEM] * len(shape),
            compiler_params=params(16),
        )(query, *taken, *carry)
        if whole and i == 0:
            *carry, pack = carry
    (attended,) = carry
    gathered = [attended] + [cross(attended, "head", k, n_head) for k in range(1, n_head)]
    shape = [SHAPE((rows, quarter), BF16)] * chunks
    if blk == 1:
        shape = [SHAPE((full, quarter), BF16)] * 2
    out = pl.pallas_call(
        functools.partial(out_kernel, blk, n_head, chunks, blk == 1),
        out_shape=shape,
        in_specs=[VMEM] * (3 * n_head + chunks + 1),
        out_specs=[VMEM] * len(shape),
        compiler_params=params(16),
    )(*gathered, *mine, *others, *xs, mod)
    return out, (valid, mod, gains), later


def solution(mesh):
    n_branch, n_seq, n_head = (mesh.shape[a] for a in ("branch", "seq", "head"))
    chunks = 2 if n_seq <= 8 else 1
    sizes = n_branch, n_seq, n_head, chunks

    def per_device(
        tokens, valid_counts, shared_qkv, shared_out, skipped_qkv, skipped_out, modulation, qk_gains
    ):
        mod = modulation.transpose(1, 0, 2)
        later = skipped_qkv.transpose(1, 0, 2), skipped_out
        forked, near, later = block(
            tokens, None, valid_counts, shared_qkv.transpose(1, 0, 2), shared_out, mod,
            qk_gains, 0, sizes, later,
        )
        valid, mod, gains = near
        (strong, sent), _, _ = block(
            None, forked, valid, *later, mod, gains, 1, sizes, None
        )
        got = swap(sent)
        rows, quarter = strong.shape
        out = pl.pallas_call(
            join_kernel,
            out_shape=SHAPE((2 * rows, quarter), BF16),
            in_specs=[VMEM] * (2 + chunks),
            out_specs=VMEM,
            compiler_params=params(8),
            name="join",
        )(strong, *forked, got)
        return out[None]

    in_specs = (
        P("seq", "head"),
        P("seq"),
        P("branch", None, "head"),
        P("head", "branch"),
        P("branch", None, "head"),
        P("head", "branch"),
        P(),
        P(),
    )
    return jax.shard_map(
        per_device,
        mesh=mesh,
        in_specs=in_specs,
        out_specs=P("branch", "seq", "head"),
        check_vma=False,
    )
```
